32 devices in a mesh: strike: 8 (over y, x, core), dip: 4 (over z).
Axes of the slice: x: 2, y: 2, z: 4, core: 2. Of those that a mesh axis runs over, the one named last changes fastest.
Arguments:
- velocity: float32 [12, 128, 1024], P(None, 'strike', 'dip'), may hold values from -6 to 6
- stress: float32 [3, 12, 128, 1024], P(None, None, 'strike', 'dip'), may hold values from -6 to 6
- shear_modulus: float32 [12, 128, 1024], P(None, 'strike', 'dip'), may hold values from 0.5 to 2
- buoyancy: float32 [12, 128, 1024], P(None, 'strike', 'dip'), may hold values from 0.5 to 2
- prestress: float32 [128, 1024], P('strike', 'dip'), may hold values from -6 to 6
- normal_stress: float32 [128, 1024], P('strike', 'dip'), may hold values from 0.5 to 2
- crit_slip: float32 [128, 1024], P('strike', 'dip'), may hold values from 0.25 to 4
- slip: float32 [128, 1024], P('strike', 'dip'), may hold values from 0 to 2
- traction: float32 [128, 1024], P('strike', 'dip'), may hold values from -6 to 6
- functional: float32 [128, 1024], P('strike', 'dip'), may hold values from -6 to 6
- flags: int32 [128, 1024], P('strike', 'dip'), may hold values 0 or 1
- history: float32 [64, 2, 1024, 128], P(None, None, ('strike', 'dip')), may hold values from -6 to 6
- kernel: bfloat16 [65, 1024, 128], P(None, ('strike', 'dip')), may hold values from -0.75 to 0.75
Outputs:
- new_velocity: float32 [12, 128, 1024], P(None, 'strike', 'dip')
- new_stress: float32 [3, 12, 128, 1024], P(None, None, 'strike', 'dip')
- new_slip: float32 [128, 1024], P('strike', 'dip')
- new_traction: float32 [128, 1024], P('strike', 'dip')
- new_functional: float32 [128, 1024], P('strike', 'dip')
The draws below stay inside these ranges and needn't reach their ends.
Inputs may be any that keep to these rules, and one draw needn't show every extreme that they name: `flags`: 1 marks a fault cell on the slip-weakening branch, 0 a stuck cell.
All inputs are finite; a program needn't handle non-finite values. No bound on the sum of `flags` on one device may be relied on, other than what follows from the above.
Results may differ from the reference program's by a relative error of at most 0.0003.
Values sent between devices are 32-bit elements; how exact they have to be, the bound alone decides.
A program may use at most 64 MiB of HBM per device.

```python
import math
import jax
import jax.numpy as jnp
from jax import lax

NZ = 12
HIST = 64
STEPS = 2
NX = 128
NY = 1024


def touch_ends(result, stream_key, low, high):
    extent = result.shape
    place = [jax.random.randint(jax.random.fold_in(stream_key, axis), (), 0, extent[axis]) for axis in range(len(extent))]
    result = result.at[tuple(place)].set(low)
    longest = extent.index(max(extent))
    place[longest] = (place[longest] + 1) % extent[longest]
    return result.at[tuple(place)].set(high)


def steps_of(stream_key, dims, pieces, smallest, top_value):
    factor_of, own = 1.0, jax.random.fold_in(stream_key, 6)
    for axis_at, blocks in pieces:
        heights = jnp.exp(jax.random.uniform(jax.random.fold_in(own, axis_at), (blocks,), jnp.float32, smallest / len(pieces), top_value / len(pieces)))
        factor_of = factor_of * jnp.repeat(heights, dims[axis_at] // blocks).reshape([-1 if axis == axis_at else 1 for axis in range(len(dims))])
    return factor_of


def gaussian(key, extent, scale, limit, pieces=(), kind=jnp.bfloat16):
    values = scale * jax.random.normal(key, extent, jnp.float32)
    if pieces:
        values = values * steps_of(key, extent, pieces, -0.22, 0.18)
    return jnp.clip(values, -limit, limit).astype(kind)


def setup_inputs(seed: int = 0) -> dict:
    keys = jax.random.split(jax.random.key(seed), 14)
    velocity = gaussian(keys[0], (NZ, NX, NY), 1.0, 6.0, ((1, 8), (2, 4)), jnp.float32)
    stress = gaussian(keys[1], (3, NZ, NX, NY), 1.0, 6.0, ((2, 8), (3, 4)), jnp.float32)
    shear_modulus = jnp.clip(jnp.exp(math.log(2.0) - 1.3862944 * jax.random.uniform(keys[2], (NZ, NX, NY), jnp.float32) ** steps_of(keys[2], (NZ, NX, NY), ((1, 8), (2, 4)), -0.2, 0.2)), 0.5, 2.0)
    buoyancy = jnp.clip(jnp.exp(math.log(2.0) - 1.3862944 * jax.random.uniform(keys[3], (NZ, NX, NY), jnp.float32) ** steps_of(keys[3], (NZ, NX, NY), ((1, 8), (2, 4)), -0.2, 0.2)), 0.5, 2.0)
    prestress = gaussian(keys[4], (NX, NY), 1.0, 6.0, ((0, 8), (1, 4)), jnp.float32)
    normal_stress = jnp.clip(jnp.exp(math.log(2.0) - 1.3862944 * jax.random.uniform(keys[5], (NX, NY), jnp.float32) ** steps_of(keys[5], (NX, NY), ((0, 8), (1, 4)), -0.2, 0.2)), 0.5, 2.0)
    crit_slip = jnp.clip(jnp.exp(math.log(4.0) - 2.7725887 * jax.random.uniform(keys[6], (NX, NY), jnp.float32) ** steps_of(keys[6], (NX, NY), ((0, 8), (1, 4)), -0.2, 0.2)), 0.25, 4.0)
    slip = jnp.clip(2.0 * jax.random.uniform(keys[7], (NX, NY), jnp.float32) ** steps_of(keys[7], (NX, NY), ((0, 8), (1, 4)), -0.2, 0.2), 0.0, 2.0)
    traction = gaussian(keys[8], (NX, NY), 1.0, 6.0, ((0, 8), (1, 4)), jnp.float32)
    functional = gaussian(keys[9], (NX, NY), 1.0, 6.0, ((0, 8), (1, 4)), jnp.float32)
    flags = touch_ends((jax.random.randint(keys[10], (NX, NY), 0, 4) < 3).astype(jnp.int32), jax.random.fold_in(keys[10], 1), 0, 1)
    history = gaussian(keys[11], (HIST, 2, NY, NX), 1.0, 6.0, ((2, 32),), jnp.float32)
    kernel = gaussian(keys[12], (HIST + 1, NY, NX), 0.125, 0.75, ((1, 32),))
    return {"velocity": velocity, "stress": stress, "shear_modulus": shear_modulus, "buoyancy": buoyancy, "prestress": prestress, "normal_stress": normal_stress, "crit_slip": crit_slip, "slip": slip, "traction": traction, "functional": functional, "flags": flags, "history": history, "kernel": kernel}


coef_near = 2.0 / 3.0
coef_far = -1.0 / 12.0
courant = 0.3
static_friction = 0.677
dynamic_friction = 0.525
damping = 0.5
time_step = 0.3


def periodic_diff(field, axis):
    return coef_near * (jnp.roll(field, -1, axis) - jnp.roll(field, 1, axis)) + coef_far * (jnp.roll(field, -2, axis) - jnp.roll(field, 2, axis))


def normal_diff(field, ghost):
    zeros = jnp.zeros_like(ghost)
    padded = jnp.concatenate([ghost, ghost, field, zeros, zeros], axis=0)
    count = field.shape[0]
    return coef_near * (padded[3:count + 3] - padded[1:count + 1]) + coef_far * (padded[4:count + 4] - padded[0:count])


def fault_update(prestress, normal_stress, crit_slip, flags, slip, stress_z, functional):
    trial = prestress + stress_z[0] + functional
    weaken = jnp.maximum(0.0, 1.0 - jnp.abs(slip) / crit_slip)
    strength = normal_stress * (dynamic_friction + (static_friction - dynamic_friction) * weaken)
    clipped = jnp.clip(trial, -strength, strength)
    traction = jnp.where(flags == 1, clipped, trial)
    rate = (trial - traction) / damping
    return traction, slip + time_step * rate


def stored_sum(kernel, history, shift):
    count = history.shape[0] - shift

    def add_term(index, carry):
        weight = lax.dynamic_index_in_dim(kernel, index + shift + 1, 0, keepdims=False).astype(jnp.float32)
        term = lax.dynamic_index_in_dim(history, index, 0, keepdims=False)
        return carry + weight[None] * term

    return lax.fori_loop(0, count, add_term, jnp.zeros_like(history[0]))


def reference(velocity, stress, shear_modulus, buoyancy, prestress, normal_stress, crit_slip, slip, traction, functional, flags, history, kernel):
    stress_x, stress_y, stress_z = stress[0], stress[1], stress[2]
    spectra = []
    for iteration in range(STEPS):
        divergence = periodic_diff(stress_x, 1) + periodic_diff(stress_y, 2) + normal_diff(stress_z, traction[None])
        velocity = velocity + courant * buoyancy * divergence
        ghost_zero = jnp.zeros_like(traction[None])
        stress_x = stress_x + courant * shear_modulus * periodic_diff(velocity, 1)
        stress_y = stress_y + courant * shear_modulus * periodic_diff(velocity, 2)
        stress_z = stress_z + courant * shear_modulus * normal_diff(velocity, ghost_zero)
        traction, slip = fault_update(prestress, normal_stress, crit_slip, flags, slip, stress_z, functional)
        spectrum = jnp.transpose(jnp.fft.fft2(slip, norm="ortho"))
        spectra = [spectrum] + spectra
        stored = stored_sum(kernel, history, iteration)
        sum_real = stored[0]
        sum_imag = stored[1]
        for offset, item in enumerate(spectra):
            weight = kernel[offset].astype(jnp.float32)
            sum_real = sum_real + weight * jnp.real(item)
            sum_imag = sum_imag + weight * jnp.imag(item)
        combined = lax.complex(sum_real, sum_imag)
        functional = jnp.real(jnp.fft.ifft2(jnp.transpose(combined), norm="ortho"))
    return velocity, jnp.stack([stress_x, stress_y, stress_z]), slip, traction, functional
```

```python
import functools
import math

import jax
import jax.numpy as jnp
import numpy as np
from jax import lax
from jax.experimental import pallas as pl
from jax.experimental.pallas import tpu as pltpu
from jax.sharding import PartitionSpec as P

STEPS = 2


coef_near = 2.0 / 3.0
coef_far = -1.0 / 12.0
courant = 0.3
static_friction = 0.677
dynamic_friction = 0.525
damping = 0.5
time_step = 0.3


def padded_2(block, sides, width):
    for axis, dim in sides:
        count = lax.axis_size(axis)
        forward = [(i, i + 1) for i in range(count - 1)]
        forward.append((count - 1, 0))
        backward = [(target, source) for source, target in forward]
        low = lax.ppermute(
            lax.slice_in_dim(block, block.shape[dim] - width, None, axis=dim), axis, forward
        )
        high = lax.ppermute(lax.slice_in_dim(block, 0, width, axis=dim), axis, backward)
        block = jnp.concatenate([low, block, high], axis=dim)
    return block


def central(padded, axis, start, count):

    def window(offset):
        return lax.slice_in_dim(padded, start + offset, start + offset + count, axis=axis)

    return coef_near * (window(1) - window(-1)) + coef_far * (window(2) - window(-2))


def normal_diff(field, ghost):
    zeros = jnp.zeros_like(ghost)
    padded = jnp.concatenate([ghost, ghost, field, zeros, zeros], axis=0)
    return central(padded, 0, 2, field.shape[0])


def fault_update(prestress, normal_stress, crit_slip, flags, slip, stress_z, functional):
    trial = prestress + stress_z[0] + functional
    weaken = jnp.maximum(0.0, 1.0 - jnp.abs(slip) / crit_slip)
    strength = normal_stress * (dynamic_friction + (static_friction - dynamic_friction) * weaken)
    clipped = jnp.clip(trial, -strength, strength)
    traction = jnp.where(flags == 1, clipped, trial)
    rate = (trial - traction) / damping
    return (traction, slip + time_step * rate)


def factor_pair(length):
    first = 1
    candidate = 1
    while candidate * candidate <= length:
        if length % candidate == 0:
            first = candidate
        candidate += 1
    return (first, length // first)


def phase_table(count_a, count_b, length, sign):
    product = lax.iota(jnp.int32, count_a)[:, None] * lax.iota(jnp.int32, count_b)[None, :] % length
    angles = sign * 2.0 * math.pi / length * product.astype(jnp.float32)
    return (jnp.cos(angles), jnp.sin(angles))


def contract(form, left, right):
    return jnp.einsum(form, left, right, precision=lax.Precision.HIGHEST)


def transform_last(real_part, imag_part, sign):
    length = real_part.shape[-1]
    outer, inner = factor_pair(length)
    leading = real_part.shape[:-1]
    real_part = real_part.reshape(leading + (outer, inner))
    imag_part = imag_part.reshape(leading + (outer, inner))
    first_cos, first_sin = phase_table(outer, outer, outer, sign)
    middle_real = contract("kt,...tq->...kq", first_cos, real_part) - contract(
        "kt,...tq->...kq", first_sin, imag_part
    )
    middle_imag = contract("kt,...tq->...kq", first_cos, imag_part) + contract(
        "kt,...tq->...kq", first_sin, real_part
    )
    twist_cos, twist_sin = phase_table(outer, inner, length, sign)
    middle_real, middle_imag = (
        middle_real * twist_cos - middle_imag * twist_sin,
        middle_real * twist_sin + middle_imag * twist_cos,
    )
    second_cos, second_sin = phase_table(inner, inner, inner, sign)
    out_real = contract("...kt,tm->...km", middle_real, second_cos) - contract(
        "...kt,tm->...km", middle_imag, second_sin
    )
    out_imag = contract("...kt,tm->...km", middle_real, second_sin) + contract(
        "...kt,tm->...km", middle_imag, second_cos
    )
    scale = 1.0 / math.sqrt(length)
    out_real = jnp.swapaxes(out_real, -1, -2).reshape(leading + (length,)) * scale
    out_imag = jnp.swapaxes(out_imag, -1, -2).reshape(leading + (length,)) * scale
    return (out_real, out_imag)


def general_body(
    velocity,
    stress,
    shear_modulus,
    buoyancy,
    prestress,
    normal_stress,
    crit_slip,
    slip,
    traction,
    functional,
    flags,
    history,
    kernel,
):
    strike_count = lax.axis_size("strike")
    dip_count = lax.axis_size("dip")
    depth, rows_x, cols_y = velocity.shape
    ky_local = history.shape[2]
    total_x = history.shape[3]
    total_y = cols_y * dip_count
    line_rows = rows_x // dip_count
    stress_x, stress_y, stress_z = (stress[0], stress[1], stress[2])
    ghost_zero = jnp.zeros((1, rows_x, cols_y), jnp.float32)
    spectra = []
    for iteration in range(STEPS):
        padded_x = padded_2(stress_x, (("strike", 1),), 2)
        padded_y = padded_2(stress_y, (("dip", 2),), 2)
        divergence = (
            central(padded_x, 1, 2, rows_x)
            + central(padded_y, 2, 2, cols_y)
            + normal_diff(stress_z, traction[None])
        )
        velocity = velocity + courant * buoyancy * divergence
        padded_v = padded_2(velocity, (("strike", 1), ("dip", 2)), 2)
        grad_x = central(padded_v[:, :, 2 : cols_y + 2], 1, 2, rows_x)
        grad_y = central(padded_v[:, 2 : rows_x + 2, :], 2, 2, cols_y)
        stress_x = stress_x + courant * shear_modulus * grad_x
        stress_y = stress_y + courant * shear_modulus * grad_y
        stress_z = stress_z + courant * shear_modulus * normal_diff(velocity, ghost_zero)
        traction, slip = fault_update(
            prestress, normal_stress, crit_slip, flags, slip, stress_z, functional
        )
        lines = lax.all_to_all(slip, "dip", split_axis=0, concat_axis=1, tiled=True)
        part_real, part_imag = transform_last(lines, jnp.zeros_like(lines), -1.0)
        stacked = jnp.stack([part_real, part_imag]).reshape(
            2, line_rows, strike_count, dip_count, ky_local
        )
        stacked = stacked.transpose(0, 2, 3, 4, 1).reshape(
            2, strike_count, dip_count, ky_local, 1, 1, line_rows
        )
        halfway = lax.all_to_all(stacked, "strike", split_axis=1, concat_axis=4, tiled=True)
        owned = lax.all_to_all(halfway, "dip", split_axis=2, concat_axis=5, tiled=True)
        owned = owned.reshape(2, ky_local, total_x)
        spec_real, spec_imag = transform_last(owned[0], owned[1], -1.0)
        spectra = [(spec_real, spec_imag)] + spectra
        weights = kernel[iteration + 1 :].astype(jnp.float32)
        stored = jnp.sum(weights[:, None] * history[: history.shape[0] - iteration], axis=0)
        sum_real = stored[0]
        sum_imag = stored[1]
        for offset, item in enumerate(spectra):
            weight = kernel[offset].astype(jnp.float32)
            sum_real = sum_real + weight * item[0]
            sum_imag = sum_imag + weight * item[1]
        back_real, back_imag = transform_last(sum_real, sum_imag, 1.0)
        leaving = jnp.stack([back_real, back_imag]).reshape(
            2, 1, 1, ky_local, strike_count, dip_count, line_rows
        )
        partway = lax.all_to_all(leaving, "strike", split_axis=4, concat_axis=1, tiled=True)
        returned = lax.all_to_all(partway, "dip", split_axis=5, concat_axis=2, tiled=True)
        returned = returned.reshape(2, total_y, line_rows).transpose(0, 2, 1)
        field_real, field_imag = transform_last(returned[0], returned[1], 1.0)
        functional = lax.all_to_all(field_real, "dip", split_axis=1, concat_axis=0, tiled=True)
    return (velocity, jnp.stack([stress_x, stress_y, stress_z]), slip, traction, functional)


LANES = 128
SUBLANES = 8
MESH = pl.DeviceIdType.MESH


def split_bf16(value):
    high = value.astype(jnp.bfloat16)
    return high, (value - high.astype(jnp.float32)).astype(jnp.bfloat16)


def split_table(table):
    table = np.asarray(table, np.float32)
    high = table.astype(jnp.bfloat16)
    return high, (table - high.astype(np.float32)).astype(jnp.bfloat16)


def strike_table(total_x):
    index = np.arange(total_x)
    angle = 2.0 * np.pi / total_x * (index[:, None] * index[None, :] % total_x)
    return np.concatenate([np.cos(angle), np.sin(angle)], axis=1) / np.sqrt(total_x)


def dip_table(strike_count, group, modes, cols, total_y):
    freq = (np.arange(strike_count)[:, None] * modes + np.arange(group)[None, :])[..., None]
    angle = 2.0 * np.pi / cols * (freq * np.arange(cols) % cols)
    cos, sin = np.cos(angle), np.sin(angle)
    top = np.concatenate([cos, sin], axis=-1)
    bottom = np.concatenate([-sin, cos], axis=-1)
    table = np.stack([top, bottom], axis=1)
    return table.reshape(strike_count * 2 * group, 2 * cols) / np.sqrt(total_y)


def twiddle_table(dip_count, modes, cols, total_y):
    freq = np.arange(dip_count)[:, None] * modes + np.arange(dip_count)[None, :]
    angle = 2.0 * np.pi / total_y * (freq[..., None] * np.arange(cols) % total_y)
    return np.stack([np.cos(angle), -np.sin(angle)], axis=1).astype(np.float32)


def dot3(left, right_high, right_low):
    high, low = split_bf16(left)
    rows = left.shape[0]
    both = jnp.dot(
        jnp.concatenate([high, low], axis=0), right_high, preferred_element_type=jnp.float32
    )
    return both[:rows] + both[rows:] + jnp.dot(high, right_low, preferred_element_type=jnp.float32)


def dot3_nt(left_high, left_low, right):
    high, low = split_bf16(right)

    def product(a, b):
        return lax.dot_general(a, b, (((1,), (1,)), ((), ())), preferred_element_type=jnp.float32)

    return product(left_high, high) + product(left_high, low) + product(left_low, high)


def rupture_kernel(
    strike_count,
    dip_count,
    vel_in,
    stress_in,
    shear,
    buoy,
    prestress,
    normal_stress,
    crit_slip,
    slip_in,
    traction_in,
    functional_in,
    flags,
    hist,
    kern,
    dip_hi,
    dip_lo,
    strike_hi,
    strike_lo,
    twiddle,
    vel,
    stress,
    slip_out,
    traction_out,
    functional_out,
    padded,
    edge_x,
    edge_y,
    halo_x,
    halo_y,
    slip_buf,
    gathered,
    send_b,
    recv_b,
    send_c,
    recv_c,
    send_d,
    recv_d,
    stored,
    weights,
    edge_sem,
    halo_sem,
    a_send,
    a_recv,
    b_send,
    b_recv,
    c_send,
    c_recv,
    d_send,
    d_recv,
):
    depth, rows, cols = vel_in.shape
    modes = hist.shape[2]
    total_x = hist.shape[3]
    stored_count = hist.shape[0]
    group = modes // dip_count
    my_s = lax.axis_index("strike")
    my_d = lax.axis_index("dip")

    def ring(me, offset, count):
        return lax.rem(me + offset + count, count)

    def remote(src, dst, send_sem, recv_sem, axis, target):
        return pltpu.make_async_remote_copy(
            src_ref=src,
            dst_ref=dst,
            send_sem=send_sem,
            recv_sem=recv_sem,
            device_id={axis: target},
            device_id_type=MESH,
        )

    lane = lax.broadcasted_iota(jnp.int32, (rows, LANES), 1)
    column = lax.broadcasted_iota(jnp.int32, (rows, cols), 1)
    lane_b = lax.broadcasted_iota(jnp.int32, (2 * group, LANES), 1) // rows

    def pack_x(turn, field):
        edge_x[turn, 0] = field[:, rows - 2 : rows, :]
        edge_x[turn, 1] = field[:, 0:2, :]

    def pack_y(turn, layer):
        low = jnp.zeros((rows, LANES), jnp.float32)
        high = jnp.zeros((rows, LANES), jnp.float32)
        for z in range(depth):
            here = lane // 2 == z
            last = layer(z)[:, cols - LANES :]
            first = layer(z)[:, :LANES]
            low = jnp.where(here, pltpu.roll(last, (2 * z + 2) % LANES, 1), low)
            high = jnp.where(here, pltpu.roll(first, 2 * z, 1) if z else first, high)
        edge_y[turn, 0] = low
        edge_y[turn, 1] = high

    def halo_copies(turn):
        copies = []
        for side, step in ((0, 1), (1, -1)):
            copies.append(
                remote(
                    edge_x.at[turn, side],
                    halo_x.at[turn, side],
                    edge_sem.at[turn, side],
                    halo_sem.at[turn, side],
                    "strike",
                    ring(my_s, step, strike_count),
                )
            )
            copies.append(
                remote(
                    edge_y.at[turn, side],
                    halo_y.at[turn, side],
                    edge_sem.at[turn, side + 2],
                    halo_sem.at[turn, side + 2],
                    "dip",
                    ring(my_d, step, dip_count),
                )
            )
        return copies

    def start_halos(turn):
        copies = halo_copies(turn)
        for copy in copies:
            copy.start()
        return copies

    def wait_halos(copies):
        for copy in copies:
            copy.wait_recv()

    def fill_padded(turn, field):
        padded[:, SUBLANES : SUBLANES + rows, :] = field[...]
        padded[:, SUBLANES - 2 : SUBLANES, :] = halo_x[turn, 0]
        padded[:, SUBLANES + rows : SUBLANES + rows + 2, :] = halo_x[turn, 1]

    def diff_x(z):
        def window(offset):
            return padded[z, SUBLANES + offset : SUBLANES + offset + rows, :]

        return coef_near * (window(1) - window(-1)) + coef_far * (window(2) - window(-2))

    def diff_y(turn, z, field):
        low = halo_y[turn, 0]
        high = halo_y[turn, 1]
        low_0, low_1 = low[:, 2 * z : 2 * z + 1], low[:, 2 * z + 1 : 2 * z + 2]
        high_0, high_1 = high[:, 2 * z : 2 * z + 1], high[:, 2 * z + 1 : 2 * z + 2]
        back_1 = jnp.where(column == 0, low_1, pltpu.roll(field, 1, 1))
        back_2 = jnp.where(
            column == 0, low_0, jnp.where(column == 1, low_1, pltpu.roll(field, 2, 1))
        )
        next_1 = jnp.where(column == cols - 1, high_0, pltpu.roll(field, cols - 1, 1))
        next_2 = jnp.where(
            column == cols - 2,
            high_0,
            jnp.where(column == cols - 1, high_1, pltpu.roll(field, cols - 2, 1)),
        )
        return coef_near * (next_1 - back_1) + coef_far * (next_2 - back_2)

    def diff_z(z, layer, ghost):
        def at(index):
            if index < 0:
                return ghost
            return layer(index) if index < depth else None

        total = None
        for offset, coef in ((1, coef_near), (-1, -coef_near), (2, coef_far), (-2, -coef_far)):
            value = at(z + offset)
            if value is not None:
                total = coef * value if total is None else total + coef * value
        return total

    def velocity_layer(turn, z, source, stress_ref, traction):
        divergence = (
            diff_x(z)
            + diff_y(turn, z, stress_ref[1, z])
            + diff_z(z, lambda i: stress_ref[2, i], traction)
        )
        vel[z] = source[z] + courant * buoy[z] * divergence

    def stress_z_layer(z, stress_ref):
        return stress_ref[2, z] + courant * shear[z] * diff_z(z, lambda i: vel[i], None)

    def stress_layers(turn, stress_ref):
        fill_padded(turn, vel)
        for z in range(depth):
            modulus = courant * shear[z]
            stress[0, z] = stress_ref[0, z] + modulus * diff_x(z)
            stress[1, z] = stress_ref[1, z] + modulus * diff_y(turn, z, vel[z])
            stress[2, z] = stress_z_layer(z, stress_ref)

    def start_gather(step, value):
        slip_buf[step] = value
        gathered[step, my_d] = value
        copies = []
        for k in range(1, dip_count):
            copy = remote(
                slip_buf.at[step],
                gathered.at[step, my_d],
                a_send.at[step, k],
                a_recv.at[step, k],
                "dip",
                ring(my_d, k, dip_count),
            )
            copy.start()
            copies.append(copy)
        return copies

    def wait_gather(step):
        for k in range(1, dip_count):
            source = ring(my_d, -k, dip_count)
            remote(
                slip_buf.at[step],
                gathered.at[step, source],
                a_send.at[step, k],
                a_recv.at[step, k],
                "dip",
                source,
            ).wait_recv()

    def exchange_start(step, axis, me, count, send, recv, send_sem, recv_sem):
        recv[step, me] = send[step, me]
        copies = []
        for k in range(1, count):
            target = ring(me, k, count)
            copy = remote(
                send.at[step, target],
                recv.at[step, me],
                send_sem.at[step, k],
                recv_sem.at[step, k],
                axis,
                target,
            )
            copy.start()
            copies.append(copy)
        return copies

    def exchange_wait(step, axis, me, count, send, recv, send_sem, recv_sem):
        for k in range(1, count):
            source = ring(me, -k, count)
            remote(
                send.at[step, source],
                recv.at[step, source],
                send_sem.at[step, k],
                recv_sem.at[step, k],
                axis,
                source,
            ).wait_recv()

    def phase(k0, dy):
        angle = 2.0 * math.pi * (k0 * dy % dip_count) / dip_count
        return round(math.cos(angle), 15), round(math.sin(angle), 15)

    def weighted(terms):
        total = None
        for coef, value in terms:
            if abs(coef) < 1e-12:
                continue
            term = value if coef == 1.0 else (-value if coef == -1.0 else coef * value)
            total = term if total is None else total + term
        return jnp.zeros((rows, cols), jnp.float32) if total is None else total

    def dip_forward(step):
        parts = [gathered[step, i] for i in range(dip_count)]
        real, imag = [], []
        for k0 in range(dip_count):
            phases = [phase(k0, dy) for dy in range(dip_count)]
            u_re = weighted([(c, part) for (c, _), part in zip(phases, parts)])
            u_im = weighted([(-s, part) for (_, s), part in zip(phases, parts)])
            t_re = twiddle[my_d, 0, k0 : k0 + 1, :]
            t_im = twiddle[my_d, 1, k0 : k0 + 1, :]
            real.append(u_re * t_re - u_im * t_im)
            imag.append(u_re * t_im + u_im * t_re)
        spare = LANES - dip_count * rows
        if spare:
            real.append(jnp.zeros((spare, cols), jnp.float32))
            imag.append(jnp.zeros((spare, cols), jnp.float32))
        both = jnp.concatenate(
            [jnp.concatenate(real, axis=0), jnp.concatenate(imag, axis=0)], axis=1
        )
        out = dot3_nt(dip_hi[...], dip_lo[...], both)
        send_b[step] = out.reshape(strike_count, 2 * group, LANES)

    def strike_forward(step):
        blocks = []
        for k0 in range(dip_count):
            block = jnp.zeros((2 * group, LANES), jnp.float32)
            for s in range(strike_count):
                shift = rows * (s - k0) % LANES
                piece = recv_b[step, s]
                block = jnp.where(
                    lane_b == s, pltpu.roll(piece, shift, 1) if shift else piece, block
                )
            blocks.append(block)
        both = dot3(jnp.concatenate(blocks, axis=0), strike_hi[...], strike_lo[...])
        both = both.reshape(dip_count, 2, group, 2 * total_x)
        real, imag = both[:, 0], both[:, 1]
        return (
            real[..., :total_x] + imag[..., total_x:],
            imag[..., :total_x] - real[..., total_x:],
        )

    def by_residue(ref, *lead):
        return jnp.stack(
            [ref[(*lead, pl.ds(k0, group, stride=dip_count), slice(None))] for k0 in range(dip_count)]
        )

    def convolve(step, spectra):
        sum_re = by_residue(stored, step * 2)
        sum_im = by_residue(stored, step * 2 + 1)
        for offset, (real, imag) in enumerate(spectra):
            weight = by_residue(weights, offset)
            sum_re = sum_re + weight * real
            sum_im = sum_im + weight * imag
        return sum_re, sum_im

    def strike_inverse(step, sum_re, sum_im):
        both = jnp.stack([sum_re, sum_im], axis=1).reshape(2 * modes, total_x)
        both = dot3(both, strike_hi[...], strike_lo[...])
        both = both.reshape(dip_count, 2, group, 2 * total_x)
        real, imag = both[:, 0], both[:, 1]
        back = jnp.stack(
            [
                real[..., :total_x] - imag[..., total_x:],
                imag[..., :total_x] + real[..., total_x:],
            ],
            axis=1,
        ).reshape(dip_count, 2 * group, total_x)
        for s in range(strike_count):
            block = jnp.zeros((2 * group, LANES), jnp.float32)
            for k0 in range(dip_count):
                shift = rows * (k0 - s) % LANES
                piece = back[k0]
                block = jnp.where(
                    lane_b == k0, pltpu.roll(piece, shift, 1) if shift else piece, block
                )
            send_c[step, s] = block

    def dip_inverse(step):
        packed = recv_c[step].reshape(strike_count * 2 * group, LANES)
        lines = packed.T[: dip_count * rows]
        out = dot3(lines, dip_hi[...], dip_lo[...])
        real, imag = [], []
        for k0 in range(dip_count):
            h_re = out[k0 * rows : (k0 + 1) * rows, :cols]
            h_im = out[k0 * rows : (k0 + 1) * rows, cols:]
            t_re = twiddle[my_d, 0, k0 : k0 + 1, :]
            t_im = twiddle[my_d, 1, k0 : k0 + 1, :]
            real.append(h_re * t_re + h_im * t_im)
            imag.append(h_im * t_re - h_re * t_im)
        for dy in range(dip_count):
            phases = [phase(k0, dy) for k0 in range(dip_count)]
            send_d[step, dy] = weighted(
                [(c, part) for (c, _), part in zip(phases, real)]
                + [(-s, part) for (_, s), part in zip(phases, imag)]
            )

    def store_history():
        zero = jnp.zeros((2, modes, total_x), jnp.float32)
        common = stored_count - STEPS + 1

        def term(t, j):
            return kern[j + t + 1].astype(jnp.float32)[None] * hist[j]

        def add(j, sums):
            return tuple(total + term(t, j) for t, total in enumerate(sums))

        sums = lax.fori_loop(0, common, add, (zero,) * STEPS)
        for t in range(STEPS):
            total = sums[t]
            for j in range(common, stored_count - t):
                total = total + term(t, j)
            stored[2 * t] = total[0]
            stored[2 * t + 1] = total[1]
            weights[t] = kern[t].astype(jnp.float32)

    b_args = ("strike", my_s, strike_count, send_b, recv_b, b_send, b_recv)
    c_args = ("strike", my_s, strike_count, send_c, recv_c, c_send, c_recv)
    d_args = ("dip", my_d, dip_count, send_d, recv_d, d_send, d_recv)

    barrier = pltpu.get_barrier_semaphore()
    for k in range(1, strike_count):
        pl.semaphore_signal(
            barrier, inc=1, device_id={"strike": ring(my_s, k, strike_count)}, device_id_type=MESH
        )
    for k in range(1, dip_count):
        pl.semaphore_signal(
            barrier, inc=1, device_id={"dip": ring(my_d, k, dip_count)}, device_id_type=MESH
        )
    pack_x(0, stress_in.at[0])
    pack_y(0, lambda z: stress_in[1, z])
    pl.semaphore_wait(barrier, strike_count + dip_count - 2)

    started = []
    halos = start_halos(0)
    started += halos
    store_history()

    traction = traction_in[...]
    slip = slip_in[...]
    functional = functional_in[...]
    spectra = []
    stress_ref = stress_in
    front = min(3, depth)
    for step in range(STEPS):
        if step == 0:
            wait_halos(halos)
            fill_padded(0, stress_in.at[0])
            for z in range(front):
                velocity_layer(0, z, vel_in, stress_in, traction)
        top = stress_z_layer(0, stress_in) if step == 0 else stress[2, 0]
        trial = prestress[...] + top
        trial = trial + functional
        weaken = jnp.maximum(0.0, 1.0 - jnp.abs(slip) / crit_slip[...])
        strength = normal_stress[...] * (
            dynamic_friction + (static_friction - dynamic_friction) * weaken
        )
        clipped = jnp.clip(trial, -strength, strength)
        previous = traction
        traction = jnp.where(flags[...] == 1, clipped, trial)
        slip = slip + time_step * ((trial - traction) / damping)
        started += start_gather(step, slip)
        last = step == STEPS - 1
        if step == 0:
            for z in range(front, depth):
                velocity_layer(0, z, vel_in, stress_in, previous)
            pack_x(1, vel)
            pack_y(1, lambda z: vel[z])
            halos = start_halos(1)
            started += halos
        wait_gather(step)
        dip_forward(step)
        started += exchange_start(step, *b_args)
        if not last:
            wait_halos(halos)
            stress_layers(2 * step + 1, stress_ref)
            stress_ref = stress
            pack_x(2 * step + 2, stress.at[0])
            pack_y(2 * step + 2, lambda z: stress[1, z])
            halos = start_halos(2 * step + 2)
            started += halos
        exchange_wait(step, *b_args)
        spectra = [strike_forward(step)] + spectra
        strike_inverse(step, *convolve(step, spectra))
        started += exchange_start(step, *c_args)
        if not last:
            wait_halos(halos)
            fill_padded(2 * step + 2, stress.at[0])
            for z in range(depth):
                velocity_layer(2 * step + 2, z, vel, stress, traction)
            pack_x(2 * step + 3, vel)
            pack_y(2 * step + 3, lambda z: vel[z])
            halos = start_halos(2 * step + 3)
            started += halos
        exchange_wait(step, *c_args)
        dip_inverse(step)
        started += exchange_start(step, *d_args)
        if not last:
            wait_halos(halos)
            stress_layers(2 * step + 3, stress)
        exchange_wait(step, *d_args)
        functional = recv_d[step, 0]
        for i in range(1, dip_count):
            functional = functional + recv_d[step, i]
    slip_out[...] = slip
    traction_out[...] = traction
    functional_out[...] = functional
    for copy in started:
        copy.wait_send()


def fits_kernel(strike_count, dip_count, rows, cols, modes, total_x):
    group = modes // dip_count
    return (
        STEPS == 2
        and strike_count > 1
        and dip_count > 1
        and modes % (dip_count * SUBLANES) == 0
        and rows % SUBLANES == 0
        and cols % LANES == 0
        and total_x == LANES
        and dip_count * rows <= LANES
        and strike_count * 2 * group <= 2 * LANES
    )


def body(*args):
    velocity, history = args[0], args[11]
    strike_count = lax.axis_size("strike")
    dip_count = lax.axis_size("dip")
    depth, rows, cols = velocity.shape
    modes, total_x = history.shape[2:]
    if not fits_kernel(strike_count, dip_count, rows, cols, modes, total_x):
        return general_body(*args)
    group = modes // dip_count
    total_y = cols * dip_count
    tables = (
        *split_table(dip_table(strike_count, group, modes, cols, total_y)),
        *split_table(strike_table(total_x)),
        twiddle_table(dip_count, modes, cols, total_y),
    )
    turns = 2 * STEPS
    f32 = jnp.float32
    dma = pltpu.SemaphoreType.DMA
    scratch = [
        pltpu.VMEM((depth, rows + 2 * SUBLANES, cols), f32),
        pltpu.VMEM((turns, 2, depth, 2, cols), f32),
        pltpu.VMEM((turns, 2, rows, LANES), f32),
        pltpu.VMEM((turns, 2, depth, 2, cols), f32),
        pltpu.VMEM((turns, 2, rows, LANES), f32),
        pltpu.VMEM((STEPS, rows, cols), f32),
        pltpu.VMEM((STEPS, dip_count, rows, cols), f32),
        pltpu.VMEM((STEPS, strike_count, 2 * group, LANES), f32),
        pltpu.VMEM((STEPS, strike_count, 2 * group, LANES), f32),
        pltpu.VMEM((STEPS, strike_count, 2 * group, LANES), f32),
        pltpu.VMEM((STEPS, strike_count, 2 * group, LANES), f32),
        pltpu.VMEM((STEPS, dip_count, rows, cols), f32),
        pltpu.VMEM((STEPS, dip_count, rows, cols), f32),
        pltpu.VMEM((2 * STEPS, modes, total_x), f32),
        pltpu.VMEM((STEPS, modes, total_x), f32),
        dma((turns, 4)),
        dma((turns, 4)),
        dma((STEPS, dip_count)),
        dma((STEPS, dip_count)),
        dma((STEPS, strike_count)),
        dma((STEPS, strike_count)),
        dma((STEPS, strike_count)),
        dma((STEPS, strike_count)),
        dma((STEPS, dip_count)),
        dma((STEPS, dip_count)),
    ]
    plane = jax.ShapeDtypeStruct((rows, cols), f32)
    vmem = pl.BlockSpec(memory_space=pltpu.VMEM)
    return pl.pallas_call(
        functools.partial(rupture_kernel, strike_count, dip_count),
        out_shape=(
            jax.ShapeDtypeStruct(velocity.shape, f32),
            jax.ShapeDtypeStruct(args[1].shape, f32),
            plane,
            plane,
            plane,
        ),
        in_specs=[vmem] * (len(args) + len(tables)),
        out_specs=(vmem,) * 5,
        scratch_shapes=scratch,
        compiler_params=pltpu.CompilerParams(collective_id=0, has_side_effects=True),
    )(*args, *[jnp.asarray(table) for table in tables])


def solution(mesh):
    return jax.shard_map(
        body,
        mesh=mesh,
        in_specs=(
            P(None, "strike", "dip"),
            P(None, None, "strike", "dip"),
            P(None, "strike", "dip"),
            P(None, "strike", "dip"),
            P("strike", "dip"),
            P("strike", "dip"),
            P("strike", "dip"),
            P("strike", "dip"),
            P("strike", "dip"),
            P("strike", "dip"),
            P("strike", "dip"),
            P(None, None, ("strike", "dip"), None),
            P(None, ("strike", "dip"), None),
        ),
        out_specs=(
            P(None, "strike", "dip"),
            P(None, None, "strike", "dip"),
            P("strike", "dip"),
            P("strike", "dip"),
            P("strike", "dip"),
        ),
        check_vma=False,
    )
```

```python
import functools
import math

import jax
import jax.numpy as jnp
import numpy as np
from jax import lax
from jax.experimental import pallas as pl
from jax.experimental.pallas import tpu as pltpu
from jax.sharding import PartitionSpec as P

STEPS = 2


coef_near = 2.0 / 3.0
coef_far = -1.0 / 12.0
courant = 0.3
static_friction = 0.677
dynamic_friction = 0.525
damping = 0.5
time_step = 0.3


def padded_2(block, sides, width):
    for axis, dim in sides:
        count = lax.axis_size(axis)
        forward = [(i, i + 1) for i in range(count - 1)]
        forward.append((count - 1, 0))
        backward = [(target, source) for source, target in forward]
        low = lax.ppermute(
            lax.slice_in_dim(block, block.shape[dim] - width, None, axis=dim), axis, forward
        )
        high = lax.ppermute(lax.slice_in_dim(block, 0, width, axis=dim), axis, backward)
        block = jnp.concatenate([low, block, high], axis=dim)
    return block


def central(padded, axis, start, count):

    def window(offset):
        return lax.slice_in_dim(padded, start + offset, start + offset + count, axis=axis)

    return coef_near * (window(1) - window(-1)) + coef_far * (window(2) - window(-2))


def normal_diff(field, ghost):
    zeros = jnp.zeros_like(ghost)
    padded = jnp.concatenate([ghost, ghost, field, zeros, zeros], axis=0)
    return central(padded, 0, 2, field.shape[0])


def fault_update(prestress, normal_stress, crit_slip, flags, slip, stress_z, functional):
    trial = prestress + stress_z[0] + functional
    weaken = jnp.maximum(0.0, 1.0 - jnp.abs(slip) / crit_slip)
    strength = normal_stress * (dynamic_friction + (static_friction - dynamic_friction) * weaken)
    clipped = jnp.clip(trial, -strength, strength)
    traction = jnp.where(flags == 1, clipped, trial)
    rate = (trial - traction) / damping
    return (traction, slip + time_step * rate)


def factor_pair(length):
    first = 1
    candidate = 1
    while candidate * candidate <= length:
        if length % candidate == 0:
            first = candidate
        candidate += 1
    return (first, length // first)


def phase_table(count_a, count_b, length, sign):
    product = lax.iota(jnp.int32, count_a)[:, None] * lax.iota(jnp.int32, count_b)[None, :] % length
    angles = sign * 2.0 * math.pi / length * product.astype(jnp.float32)
    return (jnp.cos(angles), jnp.sin(angles))


def contract(form, left, right):
    return jnp.einsum(form, left, right, precision=lax.Precision.HIGHEST)


def transform_last(real_part, imag_part, sign):
    length = real_part.shape[-1]
    outer, inner = factor_pair(length)
    leading = real_part.shape[:-1]
    real_part = real_part.reshape(leading + (outer, inner))
    imag_part = imag_part.reshape(leading + (outer, inner))
    first_cos, first_sin = phase_table(outer, outer, outer, sign)
    middle_real = contract("kt,...tq->...kq", first_cos, real_part) - contract(
        "kt,...tq->...kq", first_sin, imag_part
    )
    middle_imag = contract("kt,...tq->...kq", first_cos, imag_part) + contract(
        "kt,...tq->...kq", first_sin, real_part
    )
    twist_cos, twist_sin = phase_table(outer, inner, length, sign)
    middle_real, middle_imag = (
        middle_real * twist_cos - middle_imag * twist_sin,
        middle_real * twist_sin + middle_imag * twist_cos,
    )
    second_cos, second_sin = phase_table(inner, inner, inner, sign)
    out_real = contract("...kt,tm->...km", middle_real, second_cos) - contract(
        "...kt,tm->...km", middle_imag, second_sin
    )
    out_imag = contract("...kt,tm->...km", middle_real, second_sin) + contract(
        "...kt,tm->...km", middle_imag, second_cos
    )
    scale = 1.0 / math.sqrt(length)
    out_real = jnp.swapaxes(out_real, -1, -2).reshape(leading + (length,)) * scale
    out_imag = jnp.swapaxes(out_imag, -1, -2).reshape(leading + (length,)) * scale
    return (out_real, out_imag)


def general_body(
    velocity,
    stress,
    shear_modulus,
    buoyancy,
    prestress,
    normal_stress,
    crit_slip,
    slip,
    traction,
    functional,
    flags,
    history,
    kernel,
):
    strike_count = lax.axis_size("strike")
    dip_count = lax.axis_size("dip")
    depth, rows_x, cols_y = velocity.shape
    ky_local = history.shape[2]
    total_x = history.shape[3]
    total_y = cols_y * dip_count
    line_rows = rows_x // dip_count
    stress_x, stress_y, stress_z = (stress[0], stress[1], stress[2])
    ghost_zero = jnp.zeros((1, rows_x, cols_y), jnp.float32)
    spectra = []
    for iteration in range(STEPS):
        padded_x = padded_2(stress_x, (("strike", 1),), 2)
        padded_y = padded_2(stress_y, (("dip", 2),), 2)
        divergence = (
            central(padded_x, 1, 2, rows_x)
            + central(padded_y, 2, 2, cols_y)
            + normal_diff(stress_z, traction[None])
        )
        velocity = velocity + courant * buoyancy * divergence
        padded_v = padded_2(velocity, (("strike", 1), ("dip", 2)), 2)
        grad_x = central(padded_v[:, :, 2 : cols_y + 2], 1, 2, rows_x)
        grad_y = central(padded_v[:, 2 : rows_x + 2, :], 2, 2, cols_y)
        stress_x = stress_x + courant * shear_modulus * grad_x
        stress_y = stress_y + courant * shear_modulus * grad_y
        stress_z = stress_z + courant * shear_modulus * normal_diff(velocity, ghost_zero)
        traction, slip = fault_update(
            prestress, normal_stress, crit_slip, flags, slip, stress_z, functional
        )
        lines = lax.all_to_all(slip, "dip", split_axis=0, concat_axis=1, tiled=True)
        part_real, part_imag = transform_last(lines, jnp.zeros_like(lines), -1.0)
        stacked = jnp.stack([part_real, part_imag]).reshape(
            2, line_rows, strike_count, dip_count, ky_local
        )
        stacked = stacked.transpose(0, 2, 3, 4, 1).reshape(
            2, strike_count, dip_count, ky_local, 1, 1, line_rows
        )
        halfway = lax.all_to_all(stacked, "strike", split_axis=1, concat_axis=4, tiled=True)
        owned = lax.all_to_all(halfway, "dip", split_axis=2, concat_axis=5, tiled=True)
        owned = owned.reshape(2, ky_local, total_x)
        spec_real, spec_imag = transform_last(owned[0], owned[1], -1.0)
        spectra = [(spec_real, spec_imag)] + spectra
        weights = kernel[iteration + 1 :].astype(jnp.float32)
        stored = jnp.sum(weights[:, None] * history[: history.shape[0] - iteration], axis=0)
        sum_real = stored[0]
        sum_imag = stored[1]
        for offset, item in enumerate(spectra):
            weight = kernel[offset].astype(jnp.float32)
            sum_real = sum_real + weight * item[0]
            sum_imag = sum_imag + weight * item[1]
        back_real, back_imag = transform_last(sum_real, sum_imag, 1.0)
        leaving = jnp.stack([back_real, back_imag]).reshape(
            2, 1, 1, ky_local, strike_count, dip_count, line_rows
        )
        partway = lax.all_to_all(leaving, "strike", split_axis=4, concat_axis=1, tiled=True)
        returned = lax.all_to_all(partway, "dip", split_axis=5, concat_axis=2, tiled=True)
        returned = returned.reshape(2, total_y, line_rows).transpose(0, 2, 1)
        field_real, field_imag = transform_last(returned[0], returned[1], 1.0)
        functional = lax.all_to_all(field_real, "dip", split_axis=1, concat_axis=0, tiled=True)
    return (velocity, jnp.stack([stress_x, stress_y, stress_z]), slip, traction, functional)


LANES = 128
SUBLANES = 8
MESH = pl.DeviceIdType.MESH
INPUTS = 18
KERNEL_VMEM = 40 * 2**20
HUGE = float(np.finfo(np.float32).max)


def split_bf16(value):
    high = value.astype(jnp.bfloat16)
    return high, (value - high.astype(jnp.float32)).astype(jnp.bfloat16)


def split_table(table):
    table = np.asarray(table, np.float32)
    high = table.astype(jnp.bfloat16)
    return high, (table - high.astype(np.float32)).astype(jnp.bfloat16)


def strike_table(total_x):
    index = np.arange(total_x)
    angle = 2.0 * np.pi / total_x * (index[:, None] * index[None, :] % total_x)
    return np.concatenate([np.cos(angle), np.sin(angle)], axis=1) / np.sqrt(total_x)


def dip_table(strike_count, group, modes, cols, total_y):
    freq = (np.arange(strike_count)[:, None] * modes + np.arange(group)[None, :])[..., None]
    angle = 2.0 * np.pi / cols * (freq * np.arange(cols) % cols)
    cos, sin = np.cos(angle), np.sin(angle)
    top = np.concatenate([cos, sin], axis=-1)
    bottom = np.concatenate([-sin, cos], axis=-1)
    table = np.stack([top, bottom])
    return table.reshape(2 * strike_count * group, 2 * cols) / np.sqrt(total_y)


def twiddle_table(dip_count, modes, cols, total_y):
    freq = np.arange(dip_count)[:, None] * modes + np.arange(dip_count)[None, :]
    angle = 2.0 * np.pi / total_y * (freq[..., None] * np.arange(cols) % total_y)
    return np.stack([np.cos(angle), -np.sin(angle)], axis=1).astype(np.float32)


def dot3(left, right_high, right_low):
    high, low = split_bf16(left)
    rows = left.shape[0]
    both = jnp.dot(
        jnp.concatenate([high, low], axis=0), right_high, preferred_element_type=jnp.float32
    )
    return both[:rows] + both[rows:] + jnp.dot(high, right_low, preferred_element_type=jnp.float32)


def dot3_nt(left_high, left_low, right):
    high, low = split_bf16(right)

    def product(a, b):
        return lax.dot_general(a, b, (((1,), (1,)), ((), ())), preferred_element_type=jnp.float32)

    return product(left_high, high) + product(left_high, low) + product(left_low, high)


def rupture_kernel(strike_count, dip_count, *refs):
    sources, refs = refs[:INPUTS], refs[INPUTS:]
    results, refs = refs[:5], refs[5:]
    loaded, refs = refs[:INPUTS], refs[INPUTS:]
    (
        vel_in, stress_in, shear, buoy, prestress, normal_stress, crit_slip, slip_in, traction_in,
        functional_in, flags, hist, kern, dip_hi, dip_lo, strike_hi, strike_lo, twiddle,
    ) = loaded
    (
        vel, stress, planes_out, padded, edge_x, edge_y, halo_x, halo_y, shared, gathered, send_b,
        recv_b, send_c, recv_c, lines_out, stored, weights, load_sem, save_sem, edge_sem, halo_sem,
        a_send, a_recv, b_send, b_recv, c_send, c_recv,
    ) = refs
    depth, rows, cols = vel_in.shape
    modes = hist.shape[2]
    total_x = hist.shape[3]
    stored_count = hist.shape[0]
    group = modes // dip_count
    my_s = lax.axis_index("strike")
    my_d = lax.axis_index("dip")

    def ring(me, offset, count):
        return lax.rem(me + offset + count, count)

    def remote(src, dst, send_sem, recv_sem, target):
        return pltpu.make_async_remote_copy(
            src_ref=src,
            dst_ref=dst,
            send_sem=send_sem,
            recv_sem=recv_sem,
            device_id=target,
            device_id_type=MESH,
        )

    lane = lax.broadcasted_iota(jnp.int32, (rows, LANES), 1)
    column = lax.broadcasted_iota(jnp.int32, (rows, cols), 1)
    lane_b = lax.broadcasted_iota(jnp.int32, (group, LANES), 1) // rows

    def pack_x(turn, field):
        edge_x[turn, 0] = field[:, rows - 2 : rows, :]
        edge_x[turn, 1] = field[:, 0:2, :]

    def pack_y(turn, layer):
        low = jnp.zeros((rows, LANES), jnp.float32)
        high = jnp.zeros((rows, LANES), jnp.float32)
        for z in range(depth):
            here = lane // 2 == z
            last = layer(z)[:, cols - LANES :]
            first = layer(z)[:, :LANES]
            low = jnp.where(here, pltpu.roll(last, (2 * z + 2) % LANES, 1), low)
            high = jnp.where(here, pltpu.roll(first, 2 * z, 1) if z else first, high)
        edge_y[turn, 0] = low
        edge_y[turn, 1] = high

    def halo_copies(turn):
        copies = []
        for side, step in ((0, 1), (1, -1)):
            copies.append(
                remote(
                    edge_x.at[turn, side],
                    halo_x.at[turn, side],
                    edge_sem.at[turn, side],
                    halo_sem.at[turn, side],
                    {"strike": ring(my_s, step, strike_count)},
                )
            )
            copies.append(
                remote(
                    edge_y.at[turn, side],
                    halo_y.at[turn, side],
                    edge_sem.at[turn, side + 2],
                    halo_sem.at[turn, side + 2],
                    {"dip": ring(my_d, step, dip_count)},
                )
            )
        return copies

    def start_halos(turn):
        copies = halo_copies(turn)
        for copy in copies:
            copy.start()
        return copies

    def wait_halos(copies):
        for copy in copies:
            copy.wait_recv()

    def fill_padded(turn, field):
        padded[:, SUBLANES : SUBLANES + rows, :] = field[...]
        padded[:, SUBLANES - 2 : SUBLANES, :] = halo_x[turn, 0]
        padded[:, SUBLANES + rows : SUBLANES + rows + 2, :] = halo_x[turn, 1]

    def diff_x(z):
        def window(offset):
            return padded[z, SUBLANES + offset : SUBLANES + offset + rows, :]

        return coef_near * (window(1) - window(-1)) + coef_far * (window(2) - window(-2))

    def diff_y(turn, z, field):
        low = halo_y[turn, 0]
        high = halo_y[turn, 1]
        low_0, low_1 = low[:, 2 * z : 2 * z + 1], low[:, 2 * z + 1 : 2 * z + 2]
        high_0, high_1 = high[:, 2 * z : 2 * z + 1], high[:, 2 * z + 1 : 2 * z + 2]
        back_1 = jnp.where(column == 0, low_1, pltpu.roll(field, 1, 1))
        back_2 = jnp.where(
            column == 0, low_0, jnp.where(column == 1, low_1, pltpu.roll(field, 2, 1))
        )
        next_1 = jnp.where(column == cols - 1, high_0, pltpu.roll(field, cols - 1, 1))
        next_2 = jnp.where(
            column == cols - 2,
            high_0,
            jnp.where(column == cols - 1, high_1, pltpu.roll(field, cols - 2, 1)),
        )
        return coef_near * (next_1 - back_1) + coef_far * (next_2 - back_2)

    def diff_z(z, layer, ghost):
        def at(index):
            if index < 0:
                return ghost
            return layer(index) if index < depth else None

        total = None
        for offset, coef in ((1, coef_near), (-1, -coef_near), (2, coef_far), (-2, -coef_far)):
            value = at(z + offset)
            if value is not None:
                total = coef * value if total is None else total + coef * value
        return total

    def velocity_layer(turn, z, source, stress_ref, traction):
        divergence = (
            diff_x(z)
            + diff_y(turn, z, stress_ref[1, z])
            + diff_z(z, lambda i: stress_ref[2, i], traction)
        )
        vel[z] = source[z] + courant * buoy[z] * divergence

    def stress_z_layer(z, stress_ref):
        return stress_ref[2, z] + courant * shear[z] * diff_z(z, lambda i: vel[i], None)

    def stress_layers(turn, stress_ref):
        fill_padded(turn, vel)
        for z in range(depth):
            modulus = courant * shear[z]
            stress[0, z] = stress_ref[0, z] + modulus * diff_x(z)
            stress[1, z] = stress_ref[1, z] + modulus * diff_y(turn, z, vel[z])
            stress[2, z] = stress_z_layer(z, stress_ref)

    def start_gather(turn, value):
        shared[turn] = value
        gathered[turn, my_d] = value
        copies = []
        for k in range(1, dip_count):
            copy = remote(
                shared.at[turn],
                gathered.at[turn, my_d],
                a_send.at[turn, k],
                a_recv.at[turn, k],
                {"dip": ring(my_d, k, dip_count)},
            )
            copy.start()
            copies.append(copy)
        return copies

    def wait_gather(turn):
        for k in range(1, dip_count):
            source = ring(my_d, -k, dip_count)
            remote(
                shared.at[turn],
                gathered.at[turn, source],
                a_send.at[turn, k],
                a_recv.at[turn, k],
                {"dip": source},
            ).wait_recv()

    def start_b(step):
        recv_b[step, my_s] = send_b[step, my_s]
        copies = []
        for k in range(1, strike_count):
            target = ring(my_s, k, strike_count)
            copy = remote(
                send_b.at[step, target],
                recv_b.at[step, my_s],
                b_send.at[step, k],
                b_recv.at[step, k],
                {"strike": target},
            )
            copy.start()
            copies.append(copy)
        return copies

    def wait_b(step):
        for k in range(1, strike_count):
            source = ring(my_s, -k, strike_count)
            remote(
                send_b.at[step, source],
                recv_b.at[step, source],
                b_send.at[step, k],
                b_recv.at[step, k],
                {"strike": source},
            ).wait_recv()

    offsets = [
        (i, k) for k in reversed(range(dip_count)) for i in reversed(range(strike_count)) if i or k
    ]

    def start_c(step):
        recv_c[step, my_d, my_s] = send_c[step, my_s]
        copies = []
        for i, k in offsets:
            target_s, target_d = ring(my_s, i, strike_count), ring(my_d, k, dip_count)
            copy = remote(
                send_c.at[step, target_s],
                recv_c.at[step, my_d, my_s],
                c_send.at[step, k, i],
                c_recv.at[step, k, i],
                {"strike": target_s, "dip": target_d},
            )
            copy.start()
            copies.append(copy)
        return copies

    def wait_c(step):
        for i, k in reversed(offsets):
            source_s, source_d = ring(my_s, -i, strike_count), ring(my_d, -k, dip_count)
            remote(
                send_c.at[step, source_s],
                recv_c.at[step, source_d, source_s],
                c_send.at[step, k, i],
                c_recv.at[step, k, i],
                {"strike": source_s, "dip": source_d},
            ).wait_recv()

    def phase(k0, dy):
        angle = 2.0 * math.pi * (k0 * dy % dip_count) / dip_count
        return round(math.cos(angle), 15), round(math.sin(angle), 15)

    def weighted(terms):
        total = None
        for coef, value in terms:
            if abs(coef) < 1e-12:
                continue
            term = value if coef == 1.0 else (-value if coef == -1.0 else coef * value)
            total = term if total is None else total + term
        return jnp.zeros((rows, cols), jnp.float32) if total is None else total

    def dip_forward(step, parts):
        real, imag = [], []
        for k0 in range(dip_count):
            phases = [phase(k0, dy) for dy in range(dip_count)]
            u_re = weighted([(c, part) for (c, _), part in zip(phases, parts)])
            u_im = weighted([(-s, part) for (_, s), part in zip(phases, parts)])
            t_re = twiddle[my_d, 0, k0 : k0 + 1, :]
            t_im = twiddle[my_d, 1, k0 : k0 + 1, :]
            real.append(u_re * t_re - u_im * t_im)
            imag.append(u_re * t_im + u_im * t_re)
        both = jnp.concatenate(
            [jnp.concatenate(real * 2, axis=0), jnp.concatenate(imag * 2, axis=0)], axis=1
        )
        out = dot3_nt(dip_hi[...], dip_lo[...], both)
        out = out.reshape(2, strike_count, group, LANES)
        for s in range(strike_count):
            send_b[step, s] = jnp.where(lane_b < dip_count, out[0, s], out[1, s])

    def strike_forward(step):
        blocks = []
        for k0 in range(dip_count):
            for part in range(2):
                place = part * dip_count + k0
                block = jnp.zeros((group, LANES), jnp.float32)
                for s in range(strike_count):
                    shift = rows * (s - place) % LANES
                    piece = recv_b[step, s]
                    block = jnp.where(
                        lane_b == s, pltpu.roll(piece, shift, 1) if shift else piece, block
                    )
                blocks.append(block)
        both = dot3(jnp.concatenate(blocks, axis=0), strike_hi[...], strike_lo[...])
        both = both.reshape(dip_count, 2, group, 2 * total_x)
        real, imag = both[:, 0], both[:, 1]
        return (
            real[..., :total_x] + imag[..., total_x:],
            imag[..., :total_x] - real[..., total_x:],
        )

    def by_residue(ref, *lead):
        return jnp.stack(
            [ref[(*lead, pl.ds(k0, group, stride=dip_count), slice(None))] for k0 in range(dip_count)]
        )

    def convolve(step, spectra):
        sum_re = by_residue(stored, step * 2)
        sum_im = by_residue(stored, step * 2 + 1)
        for offset, (real, imag) in enumerate(spectra):
            weight = by_residue(weights, offset)
            sum_re = sum_re + weight * real
            sum_im = sum_im + weight * imag
        return sum_re, sum_im

    def strike_inverse(step, sum_re, sum_im):
        both = jnp.stack([sum_re, sum_im], axis=1).reshape(2 * modes, total_x)
        both = dot3(both, strike_hi[...], strike_lo[...])
        both = both.reshape(dip_count, 2, group, 2 * total_x)
        real, imag = both[:, 0], both[:, 1]
        back_re = real[..., :total_x] - imag[..., total_x:]
        back_im = imag[..., :total_x] + real[..., total_x:]
        for s in range(strike_count):
            block = jnp.zeros((group, LANES), jnp.float32)
            for part, back in enumerate((back_re, back_im)):
                for k0 in range(dip_count):
                    place = part * dip_count + k0
                    shift = rows * (place - s) % LANES
                    piece = back[k0]
                    block = jnp.where(
                        lane_b == place, pltpu.roll(piece, shift, 1) if shift else piece, block
                    )
            send_c[step, s] = block

    def dip_inverse(step):
        half = dip_count * rows
        count = strike_count * group
        real_lines, imag_lines = [], []
        for i in range(dip_count):
            lines = recv_c[step, i].reshape(count, LANES).T
            real_lines.append(lines[:half])
            imag_lines.append(lines[half:])
        out = dot3(jnp.concatenate(real_lines, axis=0), dip_hi[:count], dip_lo[:count])
        out = out + dot3(jnp.concatenate(imag_lines, axis=0), dip_hi[count:], dip_lo[count:])
        real, imag = [], []
        for k0 in range(dip_count):
            sum_re = sum_im = None
            for i in range(dip_count):
                at = i * half + k0 * rows
                h_re = out[at : at + rows, :cols]
                h_im = out[at : at + rows, cols:]
                t_re = twiddle[i, 0, k0 : k0 + 1, :]
                t_im = twiddle[i, 1, k0 : k0 + 1, :]
                term_re = h_re * t_re + h_im * t_im
                term_im = h_im * t_re - h_re * t_im
                sum_re = term_re if sum_re is None else sum_re + term_re
                sum_im = term_im if sum_im is None else sum_im + term_im
            real.append(sum_re)
            imag.append(sum_im)
        result = []
        for dy in range(dip_count):
            phases = [phase(k0, dy) for k0 in range(dip_count)]
            result.append(
                weighted(
                    [(c, part) for (c, _), part in zip(phases, real)]
                    + [(-s, part) for (_, s), part in zip(phases, imag)]
                )
            )
        return result

    def store_history():
        zero = jnp.zeros((2, modes, total_x), jnp.float32)
        common = stored_count - STEPS + 1

        def term(t, j):
            return kern[j + t + 1].astype(jnp.float32)[None] * hist[j]

        def add(j, sums):
            return tuple(total + term(t, j) for t, total in enumerate(sums))

        sums = lax.fori_loop(0, common, add, (zero,) * STEPS)
        for t in range(STEPS):
            total = sums[t]
            for j in range(common, stored_count - t):
                total = total + term(t, j)
            stored[2 * t] = total[0]
            stored[2 * t + 1] = total[1]
            weights[t] = kern[t].astype(jnp.float32)

    def bound_of(slip):
        weaken = jnp.maximum(0.0, 1.0 - jnp.abs(slip) / crit_slip[...])
        strength = normal_stress[...] * (
            dynamic_friction + (static_friction - dynamic_friction) * weaken
        )
        return jnp.where(flags[...] == 1, strength, HUGE)

    def slide(trial, bound, slip):
        traction = jnp.clip(trial, -bound, bound)
        return traction, slip + time_step * ((trial - traction) / damping)

    barrier = pltpu.get_barrier_semaphore()
    for k in range(1, strike_count):
        pl.semaphore_signal(
            barrier, inc=1, device_id={"strike": ring(my_s, k, strike_count)}, device_id_type=MESH
        )
    for k in range(1, dip_count):
        pl.semaphore_signal(
            barrier, inc=1, device_id={"dip": ring(my_d, k, dip_count)}, device_id_type=MESH
        )
    loads = [
        pltpu.make_async_copy(sources[i], loaded[i], load_sem.at[i]) for i in range(INPUTS)
    ]
    loads[1].start()
    for i in range(INPUTS):
        if i != 1:
            loads[i].start()
    loads[1].wait()
    pack_x(0, stress_in.at[0])
    pack_y(0, lambda z: stress_in[1, z])
    pl.semaphore_wait(barrier, strike_count + dip_count - 2)

    started = []
    halos = start_halos(0)
    started += halos
    for i in range(INPUTS):
        if i != 1:
            loads[i].wait()

    ghost = traction_in[...]
    front = min(3, depth)
    base = prestress[...] + functional_in[...]
    bound = bound_of(slip_in[...])
    wait_halos(halos)
    fill_padded(0, stress_in.at[0])
    for z in range(front):
        velocity_layer(0, z, vel_in, stress_in, ghost)
    traction, slip = slide(base + stress_z_layer(0, stress_in), bound, slip_in[...])
    started += start_gather(0, slip)
    for z in range(front, depth):
        velocity_layer(0, z, vel_in, stress_in, ghost)
    pack_x(1, vel)
    pack_y(1, lambda z: vel[z])
    halos = start_halos(1)
    started += halos
    started += start_gather(1, bound_of(slip))
    store_history()
    wait_gather(0)
    slips = [gathered[0, i] for i in range(dip_count)]
    dip_forward(0, slips)
    started += start_b(0)
    wait_halos(halos)
    stress_layers(1, stress_in)
    pack_x(2, stress.at[0])
    pack_y(2, lambda z: stress[1, z])
    halos = start_halos(2)
    started += halos
    wait_b(0)
    spectra = [strike_forward(0)]
    strike_inverse(0, *convolve(0, spectra))
    started += start_c(0)

    wait_halos(halos)
    fill_padded(2, stress.at[0])
    for z in range(front):
        velocity_layer(2, z, vel, stress, traction)
    started += start_gather(2, prestress[...] + stress_z_layer(0, stress))
    for z in range(front, depth):
        velocity_layer(2, z, vel, stress, traction)
    pack_x(3, vel)
    pack_y(3, lambda z: vel[z])
    halos = start_halos(3)
    started += halos
    wait_gather(1)
    wait_gather(2)
    wait_c(0)
    functionals = dip_inverse(0)
    for i in range(dip_count):
        traction, slip = slide(gathered[2, i] + functionals[i], gathered[1, i], gathered[0, i])
        lines_out[0, i] = slip
        lines_out[1, i] = traction
    dip_forward(1, [lines_out[0, i] for i in range(dip_count)])
    started += start_b(1)
    wait_halos(halos)
    stress_layers(3, stress)
    saves = [
        pltpu.make_async_copy(vel, results[0], save_sem.at[0]),
        pltpu.make_async_copy(stress, results[1], save_sem.at[1]),
    ]
    for copy in saves:
        copy.start()
    wait_b(1)
    spectra = [strike_forward(1)] + spectra
    strike_inverse(1, *convolve(1, spectra))
    started += start_c(1)
    planes_out[0] = lines_out[0, my_d]
    planes_out[1] = lines_out[1, my_d]
    for copy in started:
        copy.wait_send()
    wait_c(1)
    for i, value in enumerate(dip_inverse(1)):
        lines_out[2, i] = value
    planes_out[2] = lines_out[2, my_d]
    ends = [
        pltpu.make_async_copy(planes_out.at[i], results[2 + i], save_sem.at[2 + i]) for i in range(3)
    ]
    for copy in ends:
        copy.start()
    for copy in saves + ends:
        copy.wait()


def copy_kernel(*refs):
    sources, results, sems = refs[:5], refs[5:10], refs[10]
    saves = [pltpu.make_async_copy(sources[i], results[i], sems.at[i]) for i in range(5)]
    for save in saves:
        save.start()
    for save in saves:
        save.wait()


def fits_kernel(strike_count, dip_count, rows, cols, modes, total_x):
    group = modes // dip_count
    return (
        STEPS == 2
        and strike_count > 1
        and dip_count > 1
        and modes % (dip_count * SUBLANES) == 0
        and rows % SUBLANES == 0
        and cols % LANES == 0
        and total_x == LANES
        and 2 * dip_count * rows == LANES
        and strike_count * group <= LANES
    )


def body(*args):
    velocity, history = args[0], args[11]
    strike_count = lax.axis_size("strike")
    dip_count = lax.axis_size("dip")
    depth, rows, cols = velocity.shape
    modes, total_x = history.shape[2:]
    if not fits_kernel(strike_count, dip_count, rows, cols, modes, total_x):
        return general_body(*args)
    group = modes // dip_count
    total_y = cols * dip_count
    tables = (
        *split_table(dip_table(strike_count, group, modes, cols, total_y)),
        *split_table(strike_table(total_x)),
        twiddle_table(dip_count, modes, cols, total_y),
    )
    turns = 2 * STEPS
    f32 = jnp.float32
    dma = pltpu.SemaphoreType.DMA
    operands = (*args, *[jnp.asarray(table) for table in tables])
    shapes = (velocity.shape, args[1].shape) + ((rows, cols),) * 3
    outs = tuple(jax.ShapeDtypeStruct(shape, f32) for shape in shapes)
    scratch = [pltpu.VMEM(operand.shape, operand.dtype) for operand in operands] + [
        pltpu.VMEM(velocity.shape, f32),
        pltpu.VMEM(args[1].shape, f32),
        pltpu.VMEM((3, rows, cols), f32),
        pltpu.VMEM((depth, rows + 2 * SUBLANES, cols), f32),
        pltpu.VMEM((turns, 2, depth, 2, cols), f32),
        pltpu.VMEM((turns, 2, rows, LANES), f32),
        pltpu.VMEM((turns, 2, depth, 2, cols), f32),
        pltpu.VMEM((turns, 2, rows, LANES), f32),
        pltpu.VMEM((3, rows, cols), f32),
        pltpu.VMEM((3, dip_count, rows, cols), f32),
        pltpu.VMEM((STEPS, strike_count, group, LANES), f32),
        pltpu.VMEM((STEPS, strike_count, group, LANES), f32),
        pltpu.VMEM((STEPS, strike_count, group, LANES), f32),
        pltpu.VMEM((STEPS, dip_count, strike_count, group, LANES), f32),
        pltpu.VMEM((3, dip_count, rows, cols), f32),
        pltpu.VMEM((2 * STEPS, modes, total_x), f32),
        pltpu.VMEM((STEPS, modes, total_x), f32),
        dma((len(operands),)),
        dma((len(outs),)),
        dma((turns, 4)),
        dma((turns, 4)),
        dma((3, dip_count)),
        dma((3, dip_count)),
        dma((STEPS, strike_count)),
        dma((STEPS, strike_count)),
        dma((STEPS, dip_count, strike_count)),
        dma((STEPS, dip_count, strike_count)),
    ]
    anywhere = pl.BlockSpec(memory_space=pl.ANY)
    results = pl.pallas_call(
        functools.partial(rupture_kernel, strike_count, dip_count),
        out_shape=outs,
        in_specs=[pl.BlockSpec(memory_space=pltpu.HBM)] * len(operands),
        out_specs=(anywhere,) * len(outs),
        scratch_shapes=scratch,
        compiler_params=pltpu.CompilerParams(
            collective_id=0, has_side_effects=True, vmem_limit_bytes=KERNEL_VMEM
        ),
    )(*operands)
    return pl.pallas_call(
        copy_kernel,
        out_shape=outs,
        in_specs=[anywhere] * len(outs),
        out_specs=(anywhere,) * len(outs),
        scratch_shapes=[dma((len(outs),))],
        compiler_params=pltpu.CompilerParams(vmem_limit_bytes=KERNEL_VMEM),
    )(*results)


def solution(mesh):
    return jax.shard_map(
        body,
        mesh=mesh,
        in_specs=(
            P(None, "strike", "dip"),
            P(None, None, "strike", "dip"),
            P(None, "strike", "dip"),
            P(None, "strike", "dip"),
            P("strike", "dip"),
            P("strike", "dip"),
            P("strike", "dip"),
            P("strike", "dip"),
            P("strike", "dip"),
            P("strike", "dip"),
            P("strike", "dip"),
            P(None, None, ("strike", "dip"), None),
            P(None, ("strike", "dip"), None),
        ),
        out_specs=(
            P(None, "strike", "dip"),
            P(None, None, "strike", "dip"),
            P("strike", "dip"),
            P("strike", "dip"),
            P("strike", "dip"),
        ),
        check_vma=False,
    )
```

```python
import functools
import math

import jax
import jax.numpy as jnp
import numpy as np
from jax import lax
from jax.experimental import pallas as pl
from jax.experimental.pallas import tpu as pltpu
from jax.sharding import PartitionSpec as P

STEPS = 2


coef_near = 2.0 / 3.0
coef_far = -1.0 / 12.0
courant = 0.3
static_friction = 0.677
dynamic_friction = 0.525
damping = 0.5
time_step = 0.3


def padded_2(block, sides, width):
    for axis, dim in sides:
        count = lax.axis_size(axis)
        forward = [(i, i + 1) for i in range(count - 1)]
        forward.append((count - 1, 0))
        backward = [(target, source) for source, target in forward]
        low = lax.ppermute(
            lax.slice_in_dim(block, block.shape[dim] - width, None, axis=dim), axis, forward
        )
        high = lax.ppermute(lax.slice_in_dim(block, 0, width, axis=dim), axis, backward)
        block = jnp.concatenate([low, block, high], axis=dim)
    return block


def central(padded, axis, start, count):

    def window(offset):
        return lax.slice_in_dim(padded, start + offset, start + offset + count, axis=axis)

    return coef_near * (window(1) - window(-1)) + coef_far * (window(2) - window(-2))


def normal_diff(field, ghost):
    zeros = jnp.zeros_like(ghost)
    padded = jnp.concatenate([ghost, ghost, field, zeros, zeros], axis=0)
    return central(padded, 0, 2, field.shape[0])


def fault_update(prestress, normal_stress, crit_slip, flags, slip, stress_z, functional):
    trial = prestress + stress_z[0] + functional
    weaken = jnp.maximum(0.0, 1.0 - jnp.abs(slip) / crit_slip)
    strength = normal_stress * (dynamic_friction + (static_friction - dynamic_friction) * weaken)
    clipped = jnp.clip(trial, -strength, strength)
    traction = jnp.where(flags == 1, clipped, trial)
    rate = (trial - traction) / damping
    return (traction, slip + time_step * rate)


def factor_pair(length):
    first = 1
    candidate = 1
    while candidate * candidate <= length:
        if length % candidate == 0:
            first = candidate
        candidate += 1
    return (first, length // first)


def phase_table(count_a, count_b, length, sign):
    product = lax.iota(jnp.int32, count_a)[:, None] * lax.iota(jnp.int32, count_b)[None, :] % length
    angles = sign * 2.0 * math.pi / length * product.astype(jnp.float32)
    return (jnp.cos(angles), jnp.sin(angles))


def contract(form, left, right):
    return jnp.einsum(form, left, right, precision=lax.Precision.HIGHEST)


def transform_last(real_part, imag_part, sign):
    length = real_part.shape[-1]
    outer, inner = factor_pair(length)
    leading = real_part.shape[:-1]
    real_part = real_part.reshape(leading + (outer, inner))
    imag_part = imag_part.reshape(leading + (outer, inner))
    first_cos, first_sin = phase_table(outer, outer, outer, sign)
    middle_real = contract("kt,...tq->...kq", first_cos, real_part) - contract(
        "kt,...tq->...kq", first_sin, imag_part
    )
    middle_imag = contract("kt,...tq->...kq", first_cos, imag_part) + contract(
        "kt,...tq->...kq", first_sin, real_part
    )
    twist_cos, twist_sin = phase_table(outer, inner, length, sign)
    middle_real, middle_imag = (
        middle_real * twist_cos - middle_imag * twist_sin,
        middle_real * twist_sin + middle_imag * twist_cos,
    )
    second_cos, second_sin = phase_table(inner, inner, inner, sign)
    out_real = contract("...kt,tm->...km", middle_real, second_cos) - contract(
        "...kt,tm->...km", middle_imag, second_sin
    )
    out_imag = contract("...kt,tm->...km", middle_real, second_sin) + contract(
        "...kt,tm->...km", middle_imag, second_cos
    )
    scale = 1.0 / math.sqrt(length)
    out_real = jnp.swapaxes(out_real, -1, -2).reshape(leading + (length,)) * scale
    out_imag = jnp.swapaxes(out_imag, -1, -2).reshape(leading + (length,)) * scale
    return (out_real, out_imag)


def general_body(
    velocity,
    stress,
    shear_modulus,
    buoyancy,
    prestress,
    normal_stress,
    crit_slip,
    slip,
    traction,
    functional,
    flags,
    history,
    kernel,
):
    strike_count = lax.axis_size("strike")
    dip_count = lax.axis_size("dip")
    depth, rows_x, cols_y = velocity.shape
    ky_local = history.shape[2]
    total_x = history.shape[3]
    total_y = cols_y * dip_count
    line_rows = rows_x // dip_count
    stress_x, stress_y, stress_z = (stress[0], stress[1], stress[2])
    ghost_zero = jnp.zeros((1, rows_x, cols_y), jnp.float32)
    spectra = []
    for iteration in range(STEPS):
        padded_x = padded_2(stress_x, (("strike", 1),), 2)
        padded_y = padded_2(stress_y, (("dip", 2),), 2)
        divergence = (
            central(padded_x, 1, 2, rows_x)
            + central(padded_y, 2, 2, cols_y)
            + normal_diff(stress_z, traction[None])
        )
        velocity = velocity + courant * buoyancy * divergence
        padded_v = padded_2(velocity, (("strike", 1), ("dip", 2)), 2)
        grad_x = central(padded_v[:, :, 2 : cols_y + 2], 1, 2, rows_x)
        grad_y = central(padded_v[:, 2 : rows_x + 2, :], 2, 2, cols_y)
        stress_x = stress_x + courant * shear_modulus * grad_x
        stress_y = stress_y + courant * shear_modulus * grad_y
        stress_z = stress_z + courant * shear_modulus * normal_diff(velocity, ghost_zero)
        traction, slip = fault_update(
            prestress, normal_stress, crit_slip, flags, slip, stress_z, functional
        )
        lines = lax.all_to_all(slip, "dip", split_axis=0, concat_axis=1, tiled=True)
        part_real, part_imag = transform_last(lines, jnp.zeros_like(lines), -1.0)
        stacked = jnp.stack([part_real, part_imag]).reshape(
            2, line_rows, strike_count, dip_count, ky_local
        )
        stacked = stacked.transpose(0, 2, 3, 4, 1).reshape(
            2, strike_count, dip_count, ky_local, 1, 1, line_rows
        )
        halfway = lax.all_to_all(stacked, "strike", split_axis=1, concat_axis=4, tiled=True)
        owned = lax.all_to_all(halfway, "dip", split_axis=2, concat_axis=5, tiled=True)
        owned = owned.reshape(2, ky_local, total_x)
        spec_real, spec_imag = transform_last(owned[0], owned[1], -1.0)
        spectra = [(spec_real, spec_imag)] + spectra
        weights = kernel[iteration + 1 :].astype(jnp.float32)
        stored = jnp.sum(weights[:, None] * history[: history.shape[0] - iteration], axis=0)
        sum_real = stored[0]
        sum_imag = stored[1]
        for offset, item in enumerate(spectra):
            weight = kernel[offset].astype(jnp.float32)
            sum_real = sum_real + weight * item[0]
            sum_imag = sum_imag + weight * item[1]
        back_real, back_imag = transform_last(sum_real, sum_imag, 1.0)
        leaving = jnp.stack([back_real, back_imag]).reshape(
            2, 1, 1, ky_local, strike_count, dip_count, line_rows
        )
        partway = lax.all_to_all(leaving, "strike", split_axis=4, concat_axis=1, tiled=True)
        returned = lax.all_to_all(partway, "dip", split_axis=5, concat_axis=2, tiled=True)
        returned = returned.reshape(2, total_y, line_rows).transpose(0, 2, 1)
        field_real, field_imag = transform_last(returned[0], returned[1], 1.0)
        functional = lax.all_to_all(field_real, "dip", split_axis=1, concat_axis=0, tiled=True)
    return (velocity, jnp.stack([stress_x, stress_y, stress_z]), slip, traction, functional)


LANES = 128
SUBLANES = 8
MESH = pl.DeviceIdType.MESH
INPUTS = 18
KERNEL_VMEM = 67043328 - 1000000
HUGE = float(np.finfo(np.float32).max)


def split_bf16(value):
    high = value.astype(jnp.bfloat16)
    return high, (value - high.astype(jnp.float32)).astype(jnp.bfloat16)


def split_table(table):
    table = np.asarray(table, np.float32)
    high = table.astype(jnp.bfloat16)
    return high, (table - high.astype(np.float32)).astype(jnp.bfloat16)


def strike_table(total_x):
    index = np.arange(total_x)
    angle = 2.0 * np.pi / total_x * (index[:, None] * index[None, :] % total_x)
    return np.concatenate([np.cos(angle), np.sin(angle)], axis=1) / np.sqrt(total_x)


def dip_table(strike_count, group, modes, cols, total_y):
    freq = (np.arange(strike_count)[:, None] * modes + np.arange(group)[None, :])[..., None]
    angle = 2.0 * np.pi / cols * (freq * np.arange(cols) % cols)
    cos, sin = np.cos(angle), np.sin(angle)
    top = np.concatenate([cos, sin], axis=-1)
    bottom = np.concatenate([-sin, cos], axis=-1)
    table = np.stack([top, bottom])
    return table.reshape(2 * strike_count * group, 2 * cols) / np.sqrt(total_y)


def twiddle_table(dip_count, modes, cols, total_y):
    freq = np.arange(dip_count)[:, None] * modes + np.arange(dip_count)[None, :]
    angle = 2.0 * np.pi / total_y * (freq[..., None] * np.arange(cols) % total_y)
    return np.stack([np.cos(angle), -np.sin(angle)], axis=1).astype(np.float32)


def dot3(left, right_high, right_low):
    high, low = split_bf16(left)
    rows = left.shape[0]
    both = jnp.dot(
        jnp.concatenate([high, low], axis=0), right_high, preferred_element_type=jnp.float32
    )
    return both[:rows] + both[rows:] + jnp.dot(high, right_low, preferred_element_type=jnp.float32)


def dot3_nt(left_high, left_low, right):
    high, low = split_bf16(right)

    def product(a, b):
        return lax.dot_general(a, b, (((1,), (1,)), ((), ())), preferred_element_type=jnp.float32)

    return product(left_high, high) + product(left_high, low) + product(left_low, high)


def rupture_kernel(strike_count, dip_count, *refs):
    sources, refs = refs[:INPUTS], refs[INPUTS:]
    results, refs = refs[:5], refs[5:]
    loaded, refs = refs[:INPUTS], refs[INPUTS:]
    (
        vel_in, stress_in, shear, buoy, prestress, normal_stress, crit_slip, slip_in, traction_in,
        functional_in, flags, hist, kern, dip_hi, dip_lo, strike_hi, strike_lo, twiddle,
    ) = loaded
    (
        vel, stress, planes_out, padded, edge_x, edge_y, halo_x, halo_y, shared, gathered, send_b,
        recv_b, send_c, recv_c, lines_out, stored, weights, load_sem, save_sem, edge_sem, halo_sem,
        a_send, a_recv, b_send, b_recv, c_send, c_recv,
    ) = refs
    depth, rows, cols = vel_in.shape
    modes = hist.shape[2]
    total_x = hist.shape[3]
    stored_count = hist.shape[0]
    group = modes // dip_count
    my_s = lax.axis_index("strike")
    my_d = lax.axis_index("dip")

    def ring(me, offset, count):
        return lax.rem(me + offset + count, count)

    def remote(src, dst, send_sem, recv_sem, target):
        return pltpu.make_async_remote_copy(
            src_ref=src,
            dst_ref=dst,
            send_sem=send_sem,
            recv_sem=recv_sem,
            device_id=target,
            device_id_type=MESH,
        )

    lane = lax.broadcasted_iota(jnp.int32, (rows, LANES), 1)
    column = lax.broadcasted_iota(jnp.int32, (rows, cols), 1)
    lane_b = lax.broadcasted_iota(jnp.int32, (group, LANES), 1) // rows

    def pack_x(turn, field):
        edge_x[turn, 0] = field[:, rows - 2 : rows, :]
        edge_x[turn, 1] = field[:, 0:2, :]

    def pack_y(turn, layer):
        low = jnp.zeros((rows, LANES), jnp.float32)
        high = jnp.zeros((rows, LANES), jnp.float32)
        for z in range(depth):
            here = lane // 2 == z
            last = layer(z)[:, cols - LANES :]
            first = layer(z)[:, :LANES]
            low = jnp.where(here, pltpu.roll(last, (2 * z + 2) % LANES, 1), low)
            high = jnp.where(here, pltpu.roll(first, 2 * z, 1) if z else first, high)
        edge_y[turn, 0] = low
        edge_y[turn, 1] = high

    def halo_copies(turn):
        copies = []
        for side, step in ((0, 1), (1, -1)):
            copies.append(
                remote(
                    edge_x.at[turn, side],
                    halo_x.at[turn, side],
                    edge_sem.at[turn, side],
                    halo_sem.at[turn, side],
                    {"strike": ring(my_s, step, strike_count)},
                )
            )
            copies.append(
                remote(
                    edge_y.at[turn, side],
                    halo_y.at[turn, side],
                    edge_sem.at[turn, side + 2],
                    halo_sem.at[turn, side + 2],
                    {"dip": ring(my_d, step, dip_count)},
                )
            )
        return copies

    def start_halos(turn):
        copies = halo_copies(turn)
        for copy in copies:
            copy.start()
        return copies

    def wait_halos(copies):
        for copy in copies:
            copy.wait_recv()

    def fill_padded(turn, field):
        padded[:, SUBLANES : SUBLANES + rows, :] = field[...]
        padded[:, SUBLANES - 2 : SUBLANES, :] = halo_x[turn, 0]
        padded[:, SUBLANES + rows : SUBLANES + rows + 2, :] = halo_x[turn, 1]

    def diff_x(z):
        def window(offset):
            return padded[z, SUBLANES + offset : SUBLANES + offset + rows, :]

        return coef_near * (window(1) - window(-1)) + coef_far * (window(2) - window(-2))

    def diff_y(turn, z, field):
        low = halo_y[turn, 0]
        high = halo_y[turn, 1]
        low_0, low_1 = low[:, 2 * z : 2 * z + 1], low[:, 2 * z + 1 : 2 * z + 2]
        high_0, high_1 = high[:, 2 * z : 2 * z + 1], high[:, 2 * z + 1 : 2 * z + 2]
        back_1 = jnp.where(column == 0, low_1, pltpu.roll(field, 1, 1))
        back_2 = jnp.where(
            column == 0, low_0, jnp.where(column == 1, low_1, pltpu.roll(field, 2, 1))
        )
        next_1 = jnp.where(column == cols - 1, high_0, pltpu.roll(field, cols - 1, 1))
        next_2 = jnp.where(
            column == cols - 2,
            high_0,
            jnp.where(column == cols - 1, high_1, pltpu.roll(field, cols - 2, 1)),
        )
        return coef_near * (next_1 - back_1) + coef_far * (next_2 - back_2)

    def diff_z(z, layer, ghost):
        def at(index):
            if index < 0:
                return ghost
            return layer(index) if index < depth else None

        total = None
        for offset, coef in ((1, coef_near), (-1, -coef_near), (2, coef_far), (-2, -coef_far)):
            value = at(z + offset)
            if value is not None:
                total = coef * value if total is None else total + coef * value
        return total

    def velocity_layer(turn, z, source, stress_ref, traction):
        divergence = (
            diff_x(z)
            + diff_y(turn, z, stress_ref[1, z])
            + diff_z(z, lambda i: stress_ref[2, i], traction)
        )
        vel[z] = source[z] + courant * buoy[z] * divergence

    def stress_z_layer(z, stress_ref):
        return stress_ref[2, z] + courant * shear[z] * diff_z(z, lambda i: vel[i], None)

    def stress_layers(turn, stress_ref):
        fill_padded(turn, vel)
        for z in range(depth):
            modulus = courant * shear[z]
            stress[0, z] = stress_ref[0, z] + modulus * diff_x(z)
            stress[1, z] = stress_ref[1, z] + modulus * diff_y(turn, z, vel[z])
            stress[2, z] = stress_z_layer(z, stress_ref)

    def start_gather(turn, value):
        shared[turn] = value
        gathered[turn, my_d] = value
        copies = []
        for k in range(1, dip_count):
            copy = remote(
                shared.at[turn],
                gathered.at[turn, my_d],
                a_send.at[turn, k],
                a_recv.at[turn, k],
                {"dip": ring(my_d, k, dip_count)},
            )
            copy.start()
            copies.append(copy)
        return copies

    def wait_gather(turn):
        for k in range(1, dip_count):
            source = ring(my_d, -k, dip_count)
            remote(
                shared.at[turn],
                gathered.at[turn, source],
                a_send.at[turn, k],
                a_recv.at[turn, k],
                {"dip": source},
            ).wait_recv()

    def start_b(step):
        recv_b[step, my_s] = send_b[step, my_s]
        copies = []
        for k in range(1, strike_count):
            target = ring(my_s, k, strike_count)
            copy = remote(
                send_b.at[step, target],
                recv_b.at[step, my_s],
                b_send.at[step, k],
                b_recv.at[step, k],
                {"strike": target},
            )
            copy.start()
            copies.append(copy)
        return copies

    def wait_b(step):
        for k in range(1, strike_count):
            source = ring(my_s, -k, strike_count)
            remote(
                send_b.at[step, source],
                recv_b.at[step, source],
                b_send.at[step, k],
                b_recv.at[step, k],
                {"strike": source},
            ).wait_recv()

    offsets = [
        (i, k) for k in reversed(range(dip_count)) for i in reversed(range(strike_count)) if i or k
    ]

    def start_c(step):
        recv_c[step, my_d, my_s] = send_c[step, my_s]
        copies = []
        for i, k in offsets:
            target_s, target_d = ring(my_s, i, strike_count), ring(my_d, k, dip_count)
            copy = remote(
                send_c.at[step, target_s],
                recv_c.at[step, my_d, my_s],
                c_send.at[step, k, i],
                c_recv.at[step, k, i],
                {"strike": target_s, "dip": target_d},
            )
            copy.start()
            copies.append(copy)
        return copies

    def wait_c(step):
        for i, k in reversed(offsets):
            source_s, source_d = ring(my_s, -i, strike_count), ring(my_d, -k, dip_count)
            remote(
                send_c.at[step, source_s],
                recv_c.at[step, source_d, source_s],
                c_send.at[step, k, i],
                c_recv.at[step, k, i],
                {"strike": source_s, "dip": source_d},
            ).wait_recv()

    def phase(k0, dy):
        angle = 2.0 * math.pi * (k0 * dy % dip_count) / dip_count
        return round(math.cos(angle), 15), round(math.sin(angle), 15)

    def weighted(terms):
        total = None
        for coef, value in terms:
            if abs(coef) < 1e-12:
                continue
            term = value if coef == 1.0 else (-value if coef == -1.0 else coef * value)
            total = term if total is None else total + term
        return jnp.zeros((rows, cols), jnp.float32) if total is None else total

    def dip_forward(step, parts):
        real, imag = [], []
        for k0 in range(dip_count):
            phases = [phase(k0, dy) for dy in range(dip_count)]
            u_re = weighted([(c, part) for (c, _), part in zip(phases, parts)])
            u_im = weighted([(-s, part) for (_, s), part in zip(phases, parts)])
            t_re = twiddle[my_d, 0, k0 : k0 + 1, :]
            t_im = twiddle[my_d, 1, k0 : k0 + 1, :]
            real.append(u_re * t_re - u_im * t_im)
            imag.append(u_re * t_im + u_im * t_re)
        both = jnp.concatenate(
            [jnp.concatenate(real * 2, axis=0), jnp.concatenate(imag * 2, axis=0)], axis=1
        )
        out = dot3_nt(dip_hi[...], dip_lo[...], both)
        out = out.reshape(2, strike_count, group, LANES)
        for s in range(strike_count):
            send_b[step, s] = jnp.where(lane_b < dip_count, out[0, s], out[1, s])

    def strike_forward(step):
        blocks = []
        for k0 in range(dip_count):
            for part in range(2):
                place = part * dip_count + k0
                block = jnp.zeros((group, LANES), jnp.float32)
                for s in range(strike_count):
                    shift = rows * (s - place) % LANES
                    piece = recv_b[step, s]
                    block = jnp.where(
                        lane_b == s, pltpu.roll(piece, shift, 1) if shift else piece, block
                    )
                blocks.append(block)
        both = dot3(jnp.concatenate(blocks, axis=0), strike_hi[...], strike_lo[...])
        both = both.reshape(dip_count, 2, group, 2 * total_x)
        real, imag = both[:, 0], both[:, 1]
        return (
            real[..., :total_x] + imag[..., total_x:],
            imag[..., :total_x] - real[..., total_x:],
        )

    def by_residue(ref, *lead):
        return jnp.stack(
            [ref[(*lead, pl.ds(k0, group, stride=dip_count), slice(None))] for k0 in range(dip_count)]
        )

    def convolve(step, spectra):
        sum_re = by_residue(stored, step * 2)
        sum_im = by_residue(stored, step * 2 + 1)
        for offset, (real, imag) in enumerate(spectra):
            weight = by_residue(weights, offset)
            sum_re = sum_re + weight * real
            sum_im = sum_im + weight * imag
        return sum_re, sum_im

    def strike_inverse(step, sum_re, sum_im):
        both = jnp.stack([sum_re, sum_im], axis=1).reshape(2 * modes, total_x)
        both = dot3(both, strike_hi[...], strike_lo[...])
        both = both.reshape(dip_count, 2, group, 2 * total_x)
        real, imag = both[:, 0], both[:, 1]
        back_re = real[..., :total_x] - imag[..., total_x:]
        back_im = imag[..., :total_x] + real[..., total_x:]
        for s in range(strike_count):
            block = jnp.zeros((group, LANES), jnp.float32)
            for part, back in enumerate((back_re, back_im)):
                for k0 in range(dip_count):
                    place = part * dip_count + k0
                    shift = rows * (place - s) % LANES
                    piece = back[k0]
                    block = jnp.where(
                        lane_b == place, pltpu.roll(piece, shift, 1) if shift else piece, block
                    )
            send_c[step, s] = block

    def dip_inverse(step):
        half = dip_count * rows
        count = strike_count * group
        real_lines, imag_lines = [], []
        for i in range(dip_count):
            lines = recv_c[step, i].reshape(count, LANES).T
            real_lines.append(lines[:half])
            imag_lines.append(lines[half:])
        out = dot3(jnp.concatenate(real_lines, axis=0), dip_hi[:count], dip_lo[:count])
        out = out + dot3(jnp.concatenate(imag_lines, axis=0), dip_hi[count:], dip_lo[count:])
        real, imag = [], []
        for k0 in range(dip_count):
            sum_re = sum_im = None
            for i in range(dip_count):
                at = i * half + k0 * rows
                h_re = out[at : at + rows, :cols]
                h_im = out[at : at + rows, cols:]
                t_re = twiddle[i, 0, k0 : k0 + 1, :]
                t_im = twiddle[i, 1, k0 : k0 + 1, :]
                term_re = h_re * t_re + h_im * t_im
                term_im = h_im * t_re - h_re * t_im
                sum_re = term_re if sum_re is None else sum_re + term_re
                sum_im = term_im if sum_im is None else sum_im + term_im
            real.append(sum_re)
            imag.append(sum_im)
        result = []
        for dy in range(dip_count):
            phases = [phase(k0, dy) for k0 in range(dip_count)]
            result.append(
                weighted(
                    [(c, part) for (c, _), part in zip(phases, real)]
                    + [(-s, part) for (_, s), part in zip(phases, imag)]
                )
            )
        return result

    def store_history():
        zero = jnp.zeros((2, modes, total_x), jnp.float32)
        common = stored_count - STEPS + 1

        def term(t, j):
            return kern[j + t + 1].astype(jnp.float32)[None] * hist[j]

        def add(j, sums):
            return tuple(total + term(t, j) for t, total in enumerate(sums))

        sums = lax.fori_loop(0, common, add, (zero,) * STEPS)
        for t in range(STEPS):
            total = sums[t]
            for j in range(common, stored_count - t):
                total = total + term(t, j)
            stored[2 * t] = total[0]
            stored[2 * t + 1] = total[1]
            weights[t] = kern[t].astype(jnp.float32)

    def bound_of(slip):
        weaken = jnp.maximum(0.0, 1.0 - jnp.abs(slip) / crit_slip[...])
        strength = normal_stress[...] * (
            dynamic_friction + (static_friction - dynamic_friction) * weaken
        )
        return jnp.where(flags[...] == 1, strength, HUGE)

    def slide(trial, bound, slip):
        traction = jnp.clip(trial, -bound, bound)
        return traction, slip + time_step * ((trial - traction) / damping)

    barrier = pltpu.get_barrier_semaphore()
    for k in range(1, strike_count):
        pl.semaphore_signal(
            barrier, inc=1, device_id={"strike": ring(my_s, k, strike_count)}, device_id_type=MESH
        )
    for k in range(1, dip_count):
        pl.semaphore_signal(
            barrier, inc=1, device_id={"dip": ring(my_d, k, dip_count)}, device_id_type=MESH
        )
    loads = [
        pltpu.make_async_copy(sources[i], loaded[i], load_sem.at[i]) for i in range(INPUTS)
    ]
    loads[1].start()
    for i in range(INPUTS):
        if i != 1:
            loads[i].start()
    loads[1].wait()
    pack_x(0, stress_in.at[0])
    pack_y(0, lambda z: stress_in[1, z])
    pl.semaphore_wait(barrier, strike_count + dip_count - 2)

    started = []
    halos = start_halos(0)
    started += halos
    for i in range(INPUTS):
        if i != 1:
            loads[i].wait()

    ghost = traction_in[...]
    front = min(3, depth)
    base = prestress[...] + functional_in[...]
    bound = bound_of(slip_in[...])
    wait_halos(halos)
    fill_padded(0, stress_in.at[0])
    for z in range(front):
        velocity_layer(0, z, vel_in, stress_in, ghost)
    traction, slip = slide(base + stress_z_layer(0, stress_in), bound, slip_in[...])
    started += start_gather(0, slip)
    for z in range(front, depth):
        velocity_layer(0, z, vel_in, stress_in, ghost)
    pack_x(1, vel)
    pack_y(1, lambda z: vel[z])
    halos = start_halos(1)
    started += halos
    started += start_gather(1, bound_of(slip))
    store_history()
    wait_gather(0)
    slips = [gathered[0, i] for i in range(dip_count)]
    dip_forward(0, slips)
    started += start_b(0)
    wait_halos(halos)
    stress_layers(1, stress_in)
    pack_x(2, stress.at[0])
    pack_y(2, lambda z: stress[1, z])
    halos = start_halos(2)
    started += halos
    wait_b(0)
    spectra = [strike_forward(0)]
    strike_inverse(0, *convolve(0, spectra))
    started += start_c(0)

    wait_halos(halos)
    fill_padded(2, stress.at[0])
    for z in range(front):
        velocity_layer(2, z, vel, stress, traction)
    started += start_gather(2, prestress[...] + stress_z_layer(0, stress))
    for z in range(front, depth):
        velocity_layer(2, z, vel, stress, traction)
    pack_x(3, vel)
    pack_y(3, lambda z: vel[z])
    halos = start_halos(3)
    started += halos
    wait_gather(1)
    wait_gather(2)
    wait_c(0)
    functionals = dip_inverse(0)
    for i in range(dip_count):
        traction, slip = slide(gathered[2, i] + functionals[i], gathered[1, i], gathered[0, i])
        lines_out[0, i] = slip
        lines_out[1, i] = traction
    dip_forward(1, [lines_out[0, i] for i in range(dip_count)])
    started += start_b(1)
    wait_halos(halos)
    stress_layers(3, stress)
    saves = [
        pltpu.make_async_copy(vel, results[0], save_sem.at[0]),
        pltpu.make_async_copy(stress, results[1], save_sem.at[1]),
    ]
    for copy in saves:
        copy.start()
    wait_b(1)
    spectra = [strike_forward(1)] + spectra
    strike_inverse(1, *convolve(1, spectra))
    started += start_c(1)
    planes_out[0] = lines_out[0, my_d]
    planes_out[1] = lines_out[1, my_d]
    for copy in started:
        copy.wait_send()
    wait_c(1)
    for i, value in enumerate(dip_inverse(1)):
        lines_out[2, i] = value
    planes_out[2] = lines_out[2, my_d]
    ends = [
        pltpu.make_async_copy(planes_out.at[i], results[2 + i], save_sem.at[2 + i]) for i in range(3)
    ]
    for copy in ends:
        copy.start()
    for copy in saves + ends:
        copy.wait()


def copy_kernel(*refs):
    sources, results, sems = refs[:5], refs[5:10], refs[10]
    saves = [pltpu.make_async_copy(sources[i], results[i], sems.at[i]) for i in range(5)]
    for save in saves:
        save.start()
    for save in saves:
        save.wait()


def fits_kernel(strike_count, dip_count, rows, cols, modes, total_x):
    group = modes // dip_count
    return (
        STEPS == 2
        and strike_count > 1
        and dip_count > 1
        and modes % (dip_count * SUBLANES) == 0
        and rows % SUBLANES == 0
        and cols % LANES == 0
        and total_x == LANES
        and 2 * dip_count * rows == LANES
        and strike_count * group <= LANES
    )


def body(*args):
    velocity, history = args[0], args[11]
    strike_count = lax.axis_size("strike")
    dip_count = lax.axis_size("dip")
    depth, rows, cols = velocity.shape
    modes, total_x = history.shape[2:]
    if not fits_kernel(strike_count, dip_count, rows, cols, modes, total_x):
        return general_body(*args)
    group = modes // dip_count
    total_y = cols * dip_count
    tables = (
        *split_table(dip_table(strike_count, group, modes, cols, total_y)),
        *split_table(strike_table(total_x)),
        twiddle_table(dip_count, modes, cols, total_y),
    )
    turns = 2 * STEPS
    f32 = jnp.float32
    dma = pltpu.SemaphoreType.DMA
    operands = (*args, *[jnp.asarray(table) for table in tables])
    shapes = (velocity.shape, args[1].shape) + ((rows, cols),) * 3
    outs = tuple(jax.ShapeDtypeStruct(shape, f32) for shape in shapes)
    held = tuple(pltpu.VMEM(shape, f32) for shape in shapes)
    scratch = [pltpu.VMEM(operand.shape, operand.dtype) for operand in operands] + [
        pltpu.VMEM(velocity.shape, f32),
        pltpu.VMEM(args[1].shape, f32),
        pltpu.VMEM((3, rows, cols), f32),
        pltpu.VMEM((depth, rows + 2 * SUBLANES, cols), f32),
        pltpu.VMEM((turns, 2, depth, 2, cols), f32),
        pltpu.VMEM((turns, 2, rows, LANES), f32),
        pltpu.VMEM((turns, 2, depth, 2, cols), f32),
        pltpu.VMEM((turns, 2, rows, LANES), f32),
        pltpu.VMEM((3, rows, cols), f32),
        pltpu.VMEM((3, dip_count, rows, cols), f32),
        pltpu.VMEM((STEPS, strike_count, group, LANES), f32),
        pltpu.VMEM((STEPS, strike_count, group, LANES), f32),
        pltpu.VMEM((STEPS, strike_count, group, LANES), f32),
        pltpu.VMEM((STEPS, dip_count, strike_count, group, LANES), f32),
        pltpu.VMEM((3, dip_count, rows, cols), f32),
        pltpu.VMEM((2 * STEPS, modes, total_x), f32),
        pltpu.VMEM((STEPS, modes, total_x), f32),
        dma((len(operands),)),
        dma((len(outs),)),
        dma((turns, 4)),
        dma((turns, 4)),
        dma((3, dip_count)),
        dma((3, dip_count)),
        dma((STEPS, strike_count)),
        dma((STEPS, strike_count)),
        dma((STEPS, dip_count, strike_count)),
        dma((STEPS, dip_count, strike_count)),
    ]
    anywhere = pl.BlockSpec(memory_space=pl.ANY)
    results = pl.pallas_call(
        functools.partial(rupture_kernel, strike_count, dip_count),
        out_shape=held,
        in_specs=[pl.BlockSpec(memory_space=pltpu.HBM)] * len(operands),
        out_specs=(anywhere,) * len(outs),
        scratch_shapes=scratch,
        compiler_params=pltpu.CompilerParams(
            collective_id=0, has_side_effects=True, vmem_limit_bytes=KERNEL_VMEM
        ),
    )(*operands)
    return pl.pallas_call(
        copy_kernel,
        out_shape=outs,
        in_specs=[anywhere] * len(outs),
        out_specs=(anywhere,) * len(outs),
        scratch_shapes=[dma((len(outs),))],
        compiler_params=pltpu.CompilerParams(vmem_limit_bytes=2**20),
    )(*results)


def solution(mesh):
    return jax.shard_map(
        body,
        mesh=mesh,
        in_specs=(
            P(None, "strike", "dip"),
            P(None, None, "strike", "dip"),
            P(None, "strike", "dip"),
            P(None, "strike", "dip"),
            P("strike", "dip"),
            P("strike", "dip"),
            P("strike", "dip"),
            P("strike", "dip"),
            P("strike", "dip"),
            P("strike", "dip"),
            P("strike", "dip"),
            P(None, None, ("strike", "dip"), None),
            P(None, ("strike", "dip"), None),
        ),
        out_specs=(
            P(None, "strike", "dip"),
            P(None, None, "strike", "dip"),
            P("strike", "dip"),
            P("strike", "dip"),
            P("strike", "dip"),
        ),
        check_vma=False,
    )
```
